32 devices in a mesh: dp: 8 (over z, x), tensor: 4 (over y, core).
Axes of the slice: x: 2, y: 2, z: 4, core: 2. Of those that a mesh axis runs over, the one named last changes fastest.
Arguments:
- tokens: bfloat16 [8192, 1024], P(('dp', 'tensor')), may hold values from -6 to 6
- attn_gain: float32 [1024], replicated, may hold values from 0.5 to 1.5
- qkv_weight: bfloat16 [1024, 16, 192], P('dp', 'tensor'), may hold values from -0.1875 to 0.1875
- out_weight: bfloat16 [1024, 1024], P('tensor', 'dp'), may hold values from -4 to 4
- mlp_gain: float32 [1024], replicated, may hold values from 0.5 to 1.5
- in_weight: bfloat16 [1024, 2, 2624], P('dp', None, 'tensor'), may hold values from -0.1875 to 0.1875
- down_weight: bfloat16 [2624, 1024], P('tensor', 'dp'), may hold values from -0.125 to 0.125
- seg_lengths: int32 [8, 3], P('dp'), may hold values from 1 to 512, 1024 in all within a row
- cotangent: bfloat16 [8192, 1024], P(('dp', 'tensor')), may hold values from -12 to 12
Outputs:
- layer_out: bfloat16 [8192, 1024], P(('dp', 'tensor'))
- grad_tokens: bfloat16 [8192, 1024], P(('dp', 'tensor'))
- grad_attn_gain: float32 [1024], replicated
- grad_qkv_weight: float32 [1024, 16, 192], P('dp', 'tensor')
- grad_out_weight: float32 [1024, 1024], P('tensor', 'dp')
- grad_mlp_gain: float32 [1024], replicated
- grad_in_weight: float32 [1024, 2, 2624], P('dp', None, 'tensor')
- grad_down_weight: float32 [2624, 1024], P('tensor', 'dp')
The draws below stay inside these ranges and needn't reach their ends.
Inputs may be any that keep to these rules, and one draw needn't show every extreme that they name: `seg_lengths`: row p holds the lengths of the 3 segments that fill pack p in order; they sum to 1024 and the longest is 512.
All inputs are finite; a program needn't handle non-finite values.
Results may differ from the reference program's by a relative error of at most 0.024.
Values may be sent and summed in bfloat16 or wider, within the bound.
A program may use at most 128 MiB of HBM per device.

```python
import math
import jax
import jax.numpy as jnp
import numpy as np
from jax import lax

D = 1024
HEADS = 16
HEAD_DIM = 64
FF = 2624
PACKS = 8
PACK = 1024
TOKENS = 8192
SEG_MOST = 512
NSEG = 3


def draw_cotangent(key, part):
    places = lax.broadcasted_iota(jnp.float32, (TOKENS, D), 0) / max(TOKENS - 1, 1)
    base = jnp.clip(jax.random.normal(key, (TOKENS, D), jnp.float32), -4.0, 4.0)
    row_scale = 1.0 + 2.0 * places
    return (base * row_scale).astype(jnp.bfloat16)


def level_of(stream_key, extent, shards, smallest, largest):
    factor_of = 1.0
    for dim, shards_of in shards:
        draws = jax.random.uniform(jax.random.fold_in(jax.random.fold_in(stream_key, 6), dim), (shards_of,), jnp.float32, smallest / len(shards), largest / len(shards))
        factor_of = factor_of * jnp.repeat(jnp.exp(draws), extent[dim] // shards_of).reshape((-1,) + (1,) * (len(extent) - 1 - dim))
    return factor_of


def profile(amount, total, bound, lean):
    portions = [(1 << 20) // math.isqrt(rank ** lean) + 1 for rank in range(2, amount + 1)]
    surplus, counts = total - bound - (amount - 1), [1] * (amount - 1)
    while surplus > 0:
        free = [i for i in range(amount - 1) if counts[i] < bound]
        mass, budget = sum([portions[i] for i in free]), surplus
        for i in free:
            addition = min(bound - counts[i], max(1, budget * portions[i] // mass), surplus)
            counts[i] = counts[i] + addition
            surplus = surplus - addition
    return np.array([bound] + counts)


def ragged(stream_key, count, total, reach, slope):
    if count == 2:
        one = jax.random.randint(stream_key, (), max(1, total - reach), min(reach, total - 1) + 1)
        return jnp.stack([one, total - one])
    lengths = jnp.asarray(profile(count, total, reach, slope), jnp.int32)
    couples = (count - 1) // 2
    giver, sink = lengths[1:1 + 2 * couples:2], lengths[2:2 + 2 * couples:2]
    slack = jnp.minimum(giver - 1, reach - sink)
    passed = jax.random.randint(jax.random.fold_in(stream_key, 1), (couples,), 0, 1 << 20) % (slack + 1)
    lengths = lengths.at[1:1 + 2 * couples:2].set(giver - passed).at[2:2 + 2 * couples:2].set(sink + passed)
    return lengths[jax.random.permutation(jax.random.fold_in(stream_key, 2), count)]


def scatter_about(key, extent, deviation, reach, split=(), dtype=jnp.bfloat16):
    entries = deviation * jax.random.normal(key, extent, jnp.float32)
    if split:
        entries = entries * level_of(key, extent, split, -0.22, 0.18)
    return jnp.clip(entries, -reach, reach).astype(dtype)


def setup_inputs(seed: int = 0) -> dict:
    arg_keys = jax.random.split(jax.random.key(seed), 10)
    tokens = scatter_about(arg_keys[0], (TOKENS, D), 1.0, 6.0, ((0, 32),))
    attn_gain = jnp.clip(1.0 + 0.1 * jax.random.normal(arg_keys[1], (D,), jnp.float32), 0.5, 1.5)
    qkv_weight = scatter_about(arg_keys[2], (D, HEADS, 3 * HEAD_DIM), D ** -0.5, 0.1875, ((0, 8), (1, 4)))
    out_weight = scatter_about(arg_keys[3], (HEADS * HEAD_DIM, D), 2 ** -0.5, 4.0, ((0, 4), (1, 8)))
    mlp_gain = jnp.clip(1.0 + 0.1 * jax.random.normal(arg_keys[4], (D,), jnp.float32), 0.5, 1.5)
    in_weight = scatter_about(arg_keys[5], (D, 2, FF), D ** -0.5, 0.1875, ((0, 8), (2, 4)))
    down_weight = scatter_about(arg_keys[6], (FF, D), FF ** -0.5, 0.125, ((0, 4), (1, 8)))
    seg_lengths = jax.vmap(lambda own: ragged(own, NSEG, PACK, SEG_MOST, 2))(jax.random.split(arg_keys[7], PACKS)).reshape((PACKS, NSEG)).astype(jnp.int32)
    cotangent = draw_cotangent(jax.random.fold_in(arg_keys[9], 71), 0)
    return {"tokens": tokens, "attn_gain": attn_gain, "qkv_weight": qkv_weight, "out_weight": out_weight, "mlp_gain": mlp_gain, "in_weight": in_weight, "down_weight": down_weight, "seg_lengths": seg_lengths, "cotangent": cotangent}


NORM_EPS = 1e-05
ROPE_BASE = 160000.0
HALF_ROOT = 0.7071067811865476
MASKED_SCORE = -1e+30

@jax.custom_vjp
def low(v):
    return lax.optimization_barrier(v.astype(jnp.bfloat16)).astype(jnp.float32)

@jax.custom_vjp
def low_back(v):
    return v

def low_keep(v):
    return (low(v), None)

def low_pass(kept, grad):
    return (grad,)

def back_keep(v):
    return (v, None)

def back_low(kept, grad):
    return (low(grad),)
low.defvjp(low_keep, low_pass)
low_back.defvjp(back_keep, back_low)

def matmul(left, right):
    return jnp.dot(left, right, precision=lax.Precision.HIGHEST, preferred_element_type=jnp.float32)

def layer_norm(row_data, norm_gain):
    centered = row_data - lax.optimization_barrier(jnp.mean(row_data, axis=-1, keepdims=True))
    inverse = lax.rsqrt(lax.optimization_barrier(jnp.mean(centered * centered, axis=-1, keepdims=True)) + NORM_EPS)
    return centered * inverse * norm_gain

def gelu_exact(value_in):
    return value_in * (0.5 * (1.0 + lax.erf(value_in * HALF_ROOT)))

def segment_info(seg_lens, pack_rows):
    seg_ends = jnp.cumsum(seg_lens)
    places = lax.iota(jnp.int32, pack_rows)
    before = seg_ends[None, :] <= places[:, None]
    seg_ids = lax.optimization_barrier(jnp.sum(before.astype(jnp.int32), axis=1))
    seg_first = lax.optimization_barrier(jnp.sum(jnp.where(before, seg_lens[None, :], 0), axis=1))
    return (seg_ids, places - seg_first)

def rotary(position, head_dim):
    half_dim = head_dim // 2
    inv_freq = jnp.exp(lax.iota(jnp.float32, half_dim) * (-2.0 * math.log(ROPE_BASE) / head_dim))
    angles = position.astype(jnp.float32)[:, None] * inv_freq[None, :]
    return (jnp.cos(angles), jnp.sin(angles))

def turn(vectors, cos_table, sin_table):
    half_dim = vectors.shape[-1] // 2
    front_half = vectors[..., :half_dim]
    back_half = vectors[..., half_dim:]
    cos_part = cos_table[:, None, :]
    sin_part = sin_table[:, None, :]
    return jnp.concatenate([front_half * cos_part - back_half * sin_part, back_half * cos_part + front_half * sin_part], axis=-1)

def head_attention(same_seg, head_parts):
    query_head, key_head, value_head = head_parts
    scores = matmul(query_head, key_head.T) * HEAD_DIM ** (-0.5)
    scores = low_back(scores)
    scores = jnp.where(same_seg, scores, MASKED_SCORE)
    row_top = lax.optimization_barrier(jnp.max(scores, axis=-1, keepdims=True))
    expo = jnp.exp(scores - row_top)
    probs = expo / lax.optimization_barrier(jnp.sum(expo, axis=-1, keepdims=True))
    return matmul(low(probs), value_head)

def pack_forward(row_data, seg_lens, attn_gain, qkv_weight, out_weight, mlp_gain, in_weight, down_weight):
    pack_rows = row_data.shape[0]
    seg_ids, position = segment_info(seg_lens, pack_rows)
    same_seg = seg_ids[:, None] == seg_ids[None, :]
    cos_table, sin_table = rotary(position, HEAD_DIM)
    attn_input = low(layer_norm(row_data, attn_gain))
    mixed_proj = low_back(matmul(attn_input, qkv_weight.reshape(D, HEADS * 3 * HEAD_DIM)))
    mixed_proj = mixed_proj.reshape(pack_rows, HEADS, 3, HEAD_DIM)
    query_rows = low(turn(mixed_proj[:, :, 0], cos_table, sin_table))
    key_rows = low(turn(mixed_proj[:, :, 1], cos_table, sin_table))
    value_rows = low(mixed_proj[:, :, 2])
    one_head = jax.checkpoint(lambda head_parts: head_attention(same_seg, head_parts))
    attended = lax.map(one_head, (jnp.transpose(query_rows, (1, 0, 2)), jnp.transpose(key_rows, (1, 0, 2)), jnp.transpose(value_rows, (1, 0, 2))))
    attended = jnp.transpose(attended, (1, 0, 2)).reshape(pack_rows, HEADS * HEAD_DIM)
    attended = low(low_back(attended))
    residual = row_data + low_back(matmul(attended, out_weight))
    mlp_input = low(layer_norm(residual, mlp_gain))
    lifted = low_back(matmul(mlp_input, in_weight.reshape(D, 2 * FF))).reshape(pack_rows, 2, FF)
    activated = low(gelu_exact(lifted[:, 0]) * lifted[:, 1])
    return residual + low_back(matmul(activated, down_weight))

def reference(tokens, attn_gain, qkv_weight, out_weight, mlp_gain, in_weight, down_weight, seg_lengths, cotangent):
    params = (attn_gain.astype(jnp.float32), qkv_weight.astype(jnp.float32), out_weight.astype(jnp.float32), mlp_gain.astype(jnp.float32), in_weight.astype(jnp.float32), down_weight.astype(jnp.float32))
    row_data = tokens.astype(jnp.float32)

    def whole(all_rows, weights_all):

        def one_pack(item):
            pack_data, seg_lens = item
            return pack_forward(pack_data, seg_lens, *weights_all)
        outputs = lax.map(jax.checkpoint(one_pack), (all_rows.reshape(PACKS, PACK, D), seg_lengths))
        return outputs.reshape(TOKENS, D)
    output, pullback = jax.vjp(whole, row_data, params)
    grad_rows, grads = pullback(cotangent.astype(jnp.float32))
    return (output.astype(jnp.bfloat16), grad_rows.astype(jnp.bfloat16), grads[0], grads[1], grads[2], grads[3], grads[4], grads[5])
```

```python
import math

import jax
import jax.numpy as jnp
from jax import lax
from jax.experimental import pallas as pl
from jax.experimental.pallas import tpu as pltpu
from jax.sharding import PartitionSpec as P

NORM_EPS = 1e-05
ROPE_BASE = 160000.0
HALF_ROOT = 0.7071067811865476
INV_ROOT_TAU = 0.3989422804014327
MASKED_SCORE = -1e30


def dot_plain(left, right):
    return jnp.dot(left, right, preferred_element_type=jnp.float32)


def dot_first(left, right):
    return lax.dot_general(
        left, right, (((0,), (0,)), ((), ())), preferred_element_type=jnp.float32
    )


def dot_last(left, right):
    return lax.dot_general(
        left, right, (((1,), (1,)), ((), ())), preferred_element_type=jnp.float32
    )


MESH_ID = pl.DeviceIdType.MESH
VM = pltpu.VMEM
BF = jnp.bfloat16
F32 = jnp.float32
DMA = pltpu.SemaphoreType.DMA
SPLIT = 4


def swap_halves(wide):
    width = wide.shape[1]
    lane = lax.broadcasted_iota(jnp.int32, wide.shape, 1) % 64
    return jnp.where(lane < 32, pltpu.roll(wide, width - 32, 1), pltpu.roll(wide, 32, 1))


def attend_kernel(mixed_ref, cos_ref, sin_ref, segc_ref, segr_ref, qkv_ref, att_ref, lse_ref):
    mixed = mixed_ref[...]
    qkv_ref[...] = (mixed * cos_ref[...] + swap_halves(mixed) * sin_ref[...]).astype(BF)
    rows = mixed_ref.shape[0]
    block = 256
    for head in range(2):
        base = head * 192
        keys = qkv_ref[:, base + 64 : base + 128]
        values_t = qkv_ref[:, base + 128 : base + 192].astype(F32).T.astype(BF)

        def step(i, carry):
            start = pl.multiple_of(i * block, block)
            query = qkv_ref[pl.ds(start, block), base : base + 64] * BF(0.125)
            scores = dot_last(keys, query)
            same = segc_ref[...] == segr_ref[:, pl.ds(start, block)]
            scores = jnp.where(same, scores, MASKED_SCORE)
            top = jnp.max(scores, axis=0, keepdims=True)
            expo = jnp.exp(scores - top)
            total = jnp.sum(expo, axis=0, keepdims=True)
            weights = (expo * (1.0 / total)).astype(BF)
            out_t = dot_plain(values_t, weights)
            att_ref[pl.ds(start, block), head * 64 : head * 64 + 64] = out_t.T.astype(BF)
            lse_ref[0, head : head + 1, pl.ds(start, block)] = top + jnp.log(total)
            return carry

        lax.fori_loop(0, rows // block, step, 0)


def attend_back_kernel(qkv_ref, ga_ref, lse_ref, cos_ref, sin_ref, segc_ref, segr_ref, gm_ref, acc):
    rows = qkv_ref.shape[0]
    block = 256
    for head in range(2):
        base = head * 192
        keys = qkv_ref[:, base + 64 : base + 128]
        keys_t = keys.astype(F32).T.astype(BF)
        values = qkv_ref[:, base + 128 : base + 192]

        def step(i, carry):
            grad_k, grad_v = carry
            start = pl.multiple_of(i * block, block)
            query = qkv_ref[pl.ds(start, block), base : base + 64] * BF(0.125)
            grad_o = ga_ref[pl.ds(start, block), head * 64 : head * 64 + 64]
            scores = dot_last(keys, query)
            same = segc_ref[...] == segr_ref[:, pl.ds(start, block)]
            scores = jnp.where(same, scores, MASKED_SCORE)
            probs = jnp.exp(scores - lse_ref[0, head : head + 1, pl.ds(start, block)])
            grad_p = dot_last(values, grad_o)
            inner = jnp.sum(probs * grad_p, axis=0, keepdims=True)
            grad_s = (probs * (grad_p - inner)).astype(BF)
            grad_v = grad_v + dot_plain(probs.astype(BF), grad_o)
            grad_k = grad_k + dot_plain(grad_s, query)
            grad_q = dot_plain(keys_t, grad_s) * 0.125
            acc[pl.ds(start, block), base : base + 64] = grad_q.T
            return grad_k, grad_v

        empty = jnp.zeros((rows, 64), F32)
        grad_k, grad_v = lax.fori_loop(0, rows // block, step, (empty, empty))
        acc[:, base + 64 : base + 128] = grad_k
        acc[:, base + 128 : base + 192] = grad_v
    grads = acc[...]
    gm_ref[...] = (grads * cos_ref[...] - swap_halves(grads) * sin_ref[...]).astype(BF)


def attend(mixed, cos_wide, sin_wide, seg_col, seg_row):
    rows, cols = mixed.shape
    pairs = cols // 384
    whole = lambda p: (0, 0)
    return pl.pallas_call(
        attend_kernel,
        grid=(pairs,),
        in_specs=[
            pl.BlockSpec((rows, 384), lambda p: (0, p)),
            pl.BlockSpec((rows, 384), whole),
            pl.BlockSpec((rows, 384), whole),
            pl.BlockSpec((rows, 1), whole),
            pl.BlockSpec((1, rows), whole),
        ],
        out_specs=[
            pl.BlockSpec((rows, 384), lambda p: (0, p)),
            pl.BlockSpec((rows, 128), lambda p: (0, p)),
            pl.BlockSpec((1, 2, rows), lambda p: (p, 0, 0)),
        ],
        out_shape=[
            jax.ShapeDtypeStruct((rows, cols), BF),
            jax.ShapeDtypeStruct((rows, pairs * 128), BF),
            jax.ShapeDtypeStruct((pairs, 2, rows), F32),
        ],
        cost_estimate=pl.CostEstimate(
            flops=pairs * 2 * rows * rows * 64 * 4,
            transcendentals=pairs * 2 * rows * rows,
            bytes_accessed=rows * cols * 8,
        ),
        compiler_params=pltpu.CompilerParams(vmem_limit_bytes=48 << 20),
        name="attend",
    )(mixed, cos_wide, sin_wide, seg_col, seg_row)


def attend_back(qkv, grad_att, lse, cos_wide, sin_wide, seg_col, seg_row):
    rows, cols = qkv.shape
    pairs = cols // 384
    whole = lambda p: (0, 0)
    return pl.pallas_call(
        attend_back_kernel,
        grid=(pairs,),
        in_specs=[
            pl.BlockSpec((rows, 384), lambda p: (0, p)),
            pl.BlockSpec((rows, 128), lambda p: (0, p)),
            pl.BlockSpec((1, 2, rows), lambda p: (p, 0, 0)),
            pl.BlockSpec((rows, 384), whole),
            pl.BlockSpec((rows, 384), whole),
            pl.BlockSpec((rows, 1), whole),
            pl.BlockSpec((1, rows), whole),
        ],
        out_specs=pl.BlockSpec((rows, 384), lambda p: (0, p)),
        out_shape=jax.ShapeDtypeStruct((rows, cols), BF),
        scratch_shapes=[VM((rows, 384), F32)],
        cost_estimate=pl.CostEstimate(
            flops=pairs * 2 * rows * rows * 64 * 10,
            transcendentals=pairs * 2 * rows * rows,
            bytes_accessed=rows * cols * 8,
        ),
        compiler_params=pltpu.CompilerParams(vmem_limit_bytes=48 << 20),
        name="attend_back",
    )(qkv, grad_att, lse, cos_wide, sin_wide, seg_col, seg_row)


def remote(source, target, send_sem, recv_sem, device):
    return pltpu.make_async_remote_copy(
        src_ref=source, dst_ref=target, send_sem=send_sem, recv_sem=recv_sem,
        device_id=device, device_id_type=MESH_ID,
    )


def greet(peers):
    barrier = pltpu.get_barrier_semaphore()
    for peer in peers:
        pl.semaphore_signal(barrier, inc=1, device_id=peer, device_id_type=MESH_ID)
    pl.semaphore_wait(barrier, len(peers))


def near_peers():
    dp, mine = lax.axis_index("dp"), lax.axis_index("tensor")
    across = (mine + 2) % 4
    beside = mine + 1 - 2 * (mine % 2)
    return dp, mine, across, beside


def far_peers():
    dp, mine = lax.axis_index("dp"), lax.axis_index("tensor")
    level, side = dp // 2, dp % 2
    cross = dp + 1 - 2 * side
    ahead = [((level + k) % 4) * 2 + side for k in range(4)]
    behind = [((level + 4 - k) % 4) * 2 + side for k in range(4)]
    return dp, mine, cross, ahead, behind


class RowGather:
    sems = [DMA((SPLIT,)), DMA((SPLIT,)), DMA((SPLIT + 1,)), DMA((SPLIT + 1,)), DMA]

    def __init__(self, source, target, sems):
        self.source, self.target, self.sems_in = source, target, sems
        self.rows = source.shape[0]

    def start(self):
        dp, mine, across, beside = near_peers()
        send_y, recv_y, send_c, recv_c, own = self.sems_in
        rows, part = self.rows, self.rows // SPLIT
        self.links = []
        for j in range(SPLIT):
            link = remote(
                self.source.at[pl.ds(j * part, part)],
                self.target.at[pl.ds(mine * rows + j * part, part)],
                send_y.at[j], recv_y.at[j], (dp, across))
            link.start()
            self.links.append(link)
        self.beside = remote(
            self.source, self.target.at[pl.ds(mine * rows, rows)],
            send_c.at[SPLIT], recv_c.at[SPLIT], (dp, beside))
        self.beside.start()
        self.local = pltpu.make_async_copy(
            self.source, self.target.at[pl.ds(mine * rows, rows)], own)
        self.local.start()
        self.forwards = []

    def step(self, j):
        dp, mine, across, beside = near_peers()
        send_y, recv_y, send_c, recv_c, own = self.sems_in
        rows, part = self.rows, self.rows // SPLIT
        place = self.target.at[pl.ds(across * rows + j * part, part)]
        remote(self.source.at[pl.ds(j * part, part)], place,
               send_y.at[j], recv_y.at[j], (dp, across)).wait_recv()
        forward = remote(place, place, send_c.at[j], recv_c.at[j], (dp, beside))
        forward.start()
        self.forwards.append(forward)

    def finish(self):
        dp, mine, across, beside = near_peers()
        send_y, recv_y, send_c, recv_c, own = self.sems_in
        rows, part = self.rows, self.rows // SPLIT
        other = beside
        remote(self.source, self.target.at[pl.ds(other * rows, rows)],
               send_c.at[SPLIT], recv_c.at[SPLIT], (dp, beside)).wait_recv()
        diagonal = (beside + 2) % 4
        for j in range(SPLIT):
            place = self.target.at[pl.ds(diagonal * rows + j * part, part)]
            remote(place, place, send_c.at[j], recv_c.at[j], (dp, beside)).wait_recv()
        for link in self.links + self.forwards + [self.beside]:
            link.wait_send()
        self.local.wait()


class WeightGather:
    sems = [DMA((8,)), DMA((8,)), DMA]

    def __init__(self, source, target, sems, axis):
        self.source, self.target, self.sems_in, self.axis = source, target, sems, axis

    def place(self, index):
        size = self.source.shape[self.axis]
        window = pl.ds(pl.multiple_of(index * size, size), size)
        return self.target.at[window] if self.axis == 0 else self.target.at[:, window]

    def start(self):
        dp, mine, cross, ahead, behind = far_peers()
        send, recv, own = self.sems_in
        self.links = []
        for k in (2, 1, 3):
            link = remote(self.source, self.place(dp), send.at[k], recv.at[k], (ahead[k], mine))
            link.start()
            self.links.append(link)
        link = remote(self.source, self.place(dp), send.at[4], recv.at[4], (cross, mine))
        link.start()
        self.links.append(link)
        self.local = pltpu.make_async_copy(self.source, self.place(dp), own)
        self.local.start()

    def step(self, k):
        dp, mine, cross, ahead, behind = far_peers()
        send, recv, own = self.sems_in
        place = self.place(behind[k])
        remote(self.source, place, send.at[k], recv.at[k], (ahead[k], mine)).wait_recv()
        link = remote(place, place, send.at[4 + k], recv.at[4 + k], (cross, mine))
        link.start()
        self.links.append(link)

    def finish(self):
        dp, mine, cross, ahead, behind = far_peers()
        send, recv, own = self.sems_in
        for k in range(4):
            index = behind[k] + 1 - 2 * (dp % 2)
            place = self.place(index)
            remote(place, place, send.at[4 + k], recv.at[4 + k], (cross, mine)).wait_recv()
        for link in self.links:
            link.wait_send()
        self.local.wait()


class RowReduce:
    sems = [DMA((SPLIT + 1,)), DMA((SPLIT + 1,)), DMA((SPLIT,)), DMA((SPLIT,))]

    @staticmethod
    def scratch(rows, width):
        return [VM((rows, width), BF), VM((rows, width), BF), VM((rows, width), BF), VM((rows, width), BF)]

    def __init__(self, source, target, scratch, sems):
        self.source, self.target, self.scratch_in, self.sems_in = source, target, scratch, sems
        self.rows = target.shape[0]

    def start(self):
        dp, mine, across, beside = near_peers()
        send_c, recv_c, send_y, recv_y = self.sems_in
        far_in, near_in, sums, y_in = self.scratch_in
        rows, part = self.rows, self.rows // SPLIT
        diagonal = (beside + 2) % 4
        self.links = []
        for j in range(SPLIT):
            link = remote(
                self.source.at[pl.ds(diagonal * rows + j * part, part)],
                far_in.at[pl.ds(j * part, part)], send_c.at[j], recv_c.at[j], (dp, beside))
            link.start()
            self.links.append(link)
        link = remote(
            self.source.at[pl.ds(beside * rows, rows)], near_in,
            send_c.at[SPLIT], recv_c.at[SPLIT], (dp, beside))
        link.start()
        self.links.append(link)

    def step(self, j):
        dp, mine, across, beside = near_peers()
        send_c, recv_c, send_y, recv_y = self.sems_in
        far_in, near_in, sums, y_in = self.scratch_in
        rows, part = self.rows, self.rows // SPLIT
        window = pl.ds(j * part, part)
        self.links[j].wait_recv()
        sums[window] = (
            self.source[pl.ds(across * rows + j * part, part)].astype(F32)
            + far_in[window].astype(F32)
        ).astype(BF)
        link = remote(sums.at[window], y_in.at[window], send_y.at[j], recv_y.at[j], (dp, across))
        link.start()
        self.links.append(link)

    def finish(self):
        dp, mine, across, beside = near_peers()
        far_in, near_in, sums, y_in = self.scratch_in
        rows, part = self.rows, self.rows // SPLIT
        self.links[SPLIT].wait_recv()
        for j in range(SPLIT):
            window = pl.ds(j * part, part)
            self.links[SPLIT + 1 + j].wait_recv()
            self.target[window] = (
                self.source[pl.ds(mine * rows + j * part, part)].astype(F32)
                + near_in[window].astype(F32)
                + y_in[window].astype(F32)
            )
        for link in self.links:
            link.wait_send()


class WeightReduce:
    sems = [DMA((8,)), DMA((8,))]

    @staticmethod
    def scratch(shape):
        return [VM((4, *shape), BF), VM((4, *shape), BF), VM((4, *shape), BF)]

    def __init__(self, source, target, scratch, sems, axis):
        self.source, self.target, self.scratch_in, self.sems_in = source, target, scratch, sems
        self.axis = axis

    def window(self, index):
        size = self.target.shape[self.axis]
        window = pl.ds(pl.multiple_of(index * size, size), size)
        return (window,) if self.axis == 0 else (slice(None), window)

    def start(self):
        dp, mine, cross, ahead, behind = far_peers()
        send, recv = self.sems_in
        x_in, sums, z_in = self.scratch_in
        self.links = {}
        for k in (2, 1, 3, 0):
            index = ahead[k] + 1 - 2 * (dp % 2)
            link = remote(self.source.at[self.window(index)], x_in.at[k],
                          send.at[k], recv.at[k], (cross, mine))
            link.start()
            self.links[k] = link

    def step(self, k):
        dp, mine, cross, ahead, behind = far_peers()
        send, recv = self.sems_in
        x_in, sums, z_in = self.scratch_in
        self.links[k].wait_recv()
        sums[k] = (self.source[self.window(ahead[k])].astype(F32) + x_in[k].astype(F32)).astype(BF)
        if k:
            link = remote(sums.at[k], z_in.at[k], send.at[4 + k], recv.at[4 + k], (ahead[k], mine))
            link.start()
            self.links[4 + k] = link

    def finish(self):
        x_in, sums, z_in = self.scratch_in
        for k in (1, 2, 3):
            self.links[4 + k].wait_recv()
        self.target[...] = (
            sums[0].astype(F32) + z_in[1].astype(F32) + z_in[2].astype(F32) + z_in[3].astype(F32)
        )
        for link in self.links.values():
            link.wait_send()


def run_parts(near, far):
    dp, mine, across, beside = near_peers()
    peers = [(dp, across), (dp, beside)] if near else []
    if far:
        dp, mine, cross, ahead, behind = far_peers()
        peers += [(cross, mine)] + [(ahead[k], mine) for k in (1, 2, 3)]
    greet(peers)
    for part in near + far:
        part.start()
    for j in range(SPLIT):
        for part in near:
            part.step(j)
        for part in far:
            k = (2, 1, 3, 0)[j]
            if k or isinstance(part, WeightReduce):
                part.step(k)
    for part in near + far:
        part.finish()


def comm_call(kernel, args, outs, out_spaces, scratch, ident, name):
    return pl.pallas_call(
        kernel,
        out_shape=[jax.ShapeDtypeStruct(*out) for out in outs],
        in_specs=[pl.BlockSpec(memory_space=VM)] * len(args),
        out_specs=[pl.BlockSpec(memory_space=space) for space in out_spaces],
        scratch_shapes=scratch,
        compiler_params=pltpu.CompilerParams(
            collective_id=ident, has_side_effects=True, vmem_limit_bytes=40 << 20
        ),
        name=name,
    )(*args)


def gather_rows(ident, *arrays):
    count = len(arrays)
    per = len(RowGather.sems)

    def kernel(*refs):
        sems = refs[2 * count :]
        run_parts(
            [RowGather(refs[i], refs[count + i], sems[i * per : (i + 1) * per]) for i in range(count)], []
        )

    return comm_call(
        kernel, arrays, [((4 * a.shape[0], a.shape[1]), BF) for a in arrays],
        [pl.ANY] * count, RowGather.sems * count, ident, "gather_rows")


def gather_first(ident, rows, weights, axes):
    count = 1 + len(weights)
    per_row, per_weight = len(RowGather.sems), len(WeightGather.sems)

    def kernel(*refs):
        ins, outs, sems = refs[:count], refs[count : 2 * count], refs[2 * count :]
        near = [RowGather(ins[0], outs[0], sems[:per_row])]
        sems = sems[per_row:]
        far = [
            WeightGather(ins[1 + i], outs[1 + i], sems[i * per_weight : (i + 1) * per_weight], axes[i])
            for i in range(len(weights))
        ]
        run_parts(near, far)

    shapes = [((4 * rows.shape[0], rows.shape[1]), BF)]
    for weight, axis in zip(weights, axes):
        shape = list(weight.shape)
        shape[axis] = shape[axis] * 8
        shapes.append((tuple(shape), BF))
    return comm_call(
        kernel, (rows, *weights), shapes, [pl.ANY] * count,
        RowGather.sems + WeightGather.sems * len(weights), ident, "gather_first")


def reduce_sums(ident, partial, grads, axes):
    rows = partial.shape[0] // 4
    count = 1 + len(grads)
    shapes = [((rows, partial.shape[1]), F32)]
    scratch = RowReduce.scratch(rows, partial.shape[1]) + RowReduce.sems
    for grad, axis in zip(grads, axes):
        shape = list(grad.shape)
        shape[axis] = shape[axis] // 8
        shapes.append((tuple(shape), F32))
        scratch = scratch + WeightReduce.scratch(tuple(shape)) + WeightReduce.sems

    def kernel(*refs):
        ins, outs, rest = refs[:count], refs[count : 2 * count], refs[2 * count :]
        near = [RowReduce(ins[0], outs[0], rest[:4], rest[4:8])]
        far = []
        for i in range(len(grads)):
            mine = rest[8 + 5 * i : 13 + 5 * i]
            far.append(WeightReduce(ins[1 + i], outs[1 + i], mine[:3], mine[3:], axes[i]))
        run_parts(near, far)

    return comm_call(kernel, (partial, *grads), shapes, [VM] * count, scratch, ident, "reduce_sums")


def sum_gains_kernel(part_ref, out_ref, near_in, mid, far_in, send_n, recv_n, send_f, recv_f):
    dp, mine = lax.axis_index("dp"), lax.axis_index("tensor")
    near = [(dp, (mine + k) % 4) for k in range(1, 4)]
    far = [((dp + k) % 8, mine) for k in range(1, 8)]
    greet(near + far)
    links = []
    for k in range(3):
        link = remote(part_ref, near_in.at[k], send_n.at[k], recv_n.at[k], near[k])
        link.start()
        links.append(link)
    for link in links:
        link.wait_recv()
    mid[...] = part_ref[...] + near_in[0] + near_in[1] + near_in[2]
    more = []
    for k in range(7):
        link = remote(mid, far_in.at[k], send_f.at[k], recv_f.at[k], far[k])
        link.start()
        more.append(link)
    total = mid[...]
    for k in range(7):
        more[k].wait_recv()
        total = total + far_in[k]
    out_ref[...] = total
    for link in links + more:
        link.wait_send()


def sum_gains(ident, parts):
    shape = parts.shape
    return comm_call(
        sum_gains_kernel, (parts,), [(shape, F32)], [VM],
        [VM((3, *shape), F32), VM(shape, F32), VM((7, *shape), F32),
         DMA((3,)), DMA((3,)), DMA((7,)), DMA((7,))], ident, "sum_gains")[0]


def layer_norm(row_data, norm_gain):
    centered = row_data - jnp.mean(row_data, axis=-1, keepdims=True)
    inverse = lax.rsqrt(jnp.mean(centered * centered, axis=-1, keepdims=True) + NORM_EPS)
    unit_rows = centered * inverse
    return (unit_rows * norm_gain, unit_rows, inverse)


def norm_back(grad_normed, unit_rows, inverse, norm_gain):
    scaled = grad_normed * norm_gain
    grad_rows = inverse * (
        scaled
        - jnp.mean(scaled, axis=-1, keepdims=True)
        - unit_rows * jnp.mean(scaled * unit_rows, axis=-1, keepdims=True)
    )
    return (grad_rows, jnp.sum(grad_normed * unit_rows, axis=0))


def gelu_parts(value_in):
    normal_cdf = 0.5 * (1.0 + lax.erf(value_in * HALF_ROOT))
    slope = normal_cdf + value_in * INV_ROOT_TAU * jnp.exp(-0.5 * value_in * value_in)
    return (value_in * normal_cdf, slope)


def segment_info(seg_lens, pack_rows):
    seg_ends = jnp.cumsum(seg_lens)
    places = lax.iota(jnp.int32, pack_rows)
    before = seg_ends[None, :] <= places[:, None]
    seg_ids = jnp.sum(before.astype(jnp.int32), axis=1)
    seg_first = jnp.sum(jnp.where(before, seg_lens[None, :], 0), axis=1)
    return (seg_ids, places - seg_first)


def rotary(position, head_dim):
    half_dim = head_dim // 2
    inv_freq = jnp.exp(lax.iota(jnp.float32, half_dim) * (-2.0 * math.log(ROPE_BASE) / head_dim))
    angles = position.astype(jnp.float32)[:, None] * inv_freq[None, :]
    return (jnp.cos(angles), jnp.sin(angles))


def turn(vectors, cos_table, sin_table):
    half_dim = vectors.shape[-1] // 2
    front_half = vectors[..., :half_dim]
    back_half = vectors[..., half_dim:]
    cos_part = cos_table[:, None, :]
    sin_part = sin_table[:, None, :]
    return jnp.concatenate(
        [
            front_half * cos_part - back_half * sin_part,
            back_half * cos_part + front_half * sin_part,
        ],
        axis=-1,
    )


def turn_back(grads_in, cos_table, sin_table):
    half_dim = grads_in.shape[-1] // 2
    front_half = grads_in[..., :half_dim]
    back_half = grads_in[..., half_dim:]
    cos_part = cos_table[:, None, :]
    sin_part = sin_table[:, None, :]
    return jnp.concatenate(
        [
            front_half * cos_part + back_half * sin_part,
            back_half * cos_part - front_half * sin_part,
        ],
        axis=-1,
    )


def block_scores(query_part, key_part, seg_query, seg_key, score_scale):
    scores = (
        jnp.einsum("qhd,khd->hqk", query_part, key_part, preferred_element_type=jnp.float32)
        * score_scale
    )
    return jnp.where((seg_query[:, None] == seg_key[None, :])[None], scores, MASKED_SCORE)


def attention_forward(query_rows, key_rows, value_rows, seg_ids, query_block, score_scale):
    pack_rows, heads_local, head_dim = query_rows.shape
    block_count = pack_rows // query_block

    def one_block(block_index):
        query_start = block_index * query_block
        query_part = lax.dynamic_slice_in_dim(query_rows, query_start, query_block, 0)
        seg_query = lax.dynamic_slice_in_dim(seg_ids, query_start, query_block, 0)
        scores = block_scores(query_part, key_rows, seg_query, seg_ids, score_scale)
        row_top = jnp.max(scores, axis=-1, keepdims=True)
        expo = jnp.exp(scores - row_top)
        row_total = jnp.sum(expo, axis=-1, keepdims=True)
        weights = (expo / row_total).astype(jnp.bfloat16)
        result = jnp.einsum("hqk,khd->qhd", weights, value_rows, preferred_element_type=jnp.float32)
        return (result, (row_top + jnp.log(row_total))[..., 0])

    results, log_totals = lax.map(one_block, jnp.arange(block_count, dtype=jnp.int32))
    return (results.reshape(pack_rows, heads_local, head_dim), log_totals)


def attention_backward(
    query_rows, key_rows, value_rows, grad_attended, log_totals, seg_ids, query_block, score_scale
):
    pack_rows, heads_local, head_dim = query_rows.shape
    block_count = pack_rows // query_block

    def block_step(running, block_index):
        grad_keys, grad_values = running
        query_start = block_index * query_block
        query_part = lax.dynamic_slice_in_dim(query_rows, query_start, query_block, 0)
        grad_part = lax.dynamic_slice_in_dim(grad_attended, query_start, query_block, 0)
        seg_query = lax.dynamic_slice_in_dim(seg_ids, query_start, query_block, 0)
        scores = block_scores(query_part, key_rows, seg_query, seg_ids, score_scale)
        probs = jnp.exp(scores - log_totals[block_index][..., None])
        grad_probs = jnp.einsum(
            "qhd,khd->hqk", grad_part, value_rows, preferred_element_type=jnp.float32
        )
        inner = jnp.sum(probs * grad_probs, axis=-1, keepdims=True)
        grad_scores = (probs * (grad_probs - inner)).astype(jnp.bfloat16) * score_scale
        grad_query_part = jnp.einsum(
            "hqk,khd->qhd", grad_scores, key_rows, preferred_element_type=jnp.float32
        )
        grad_key_part = jnp.einsum(
            "hqk,qhd->khd", grad_scores, query_part, preferred_element_type=jnp.float32
        )
        grad_value_part = jnp.einsum(
            "hqk,qhd->khd",
            probs.astype(jnp.bfloat16),
            grad_part,
            preferred_element_type=jnp.float32,
        )
        grad_keys = grad_keys + grad_key_part
        grad_values = grad_values + grad_value_part
        return ((grad_keys, grad_values), grad_query_part)

    empty_grad = jnp.zeros(query_rows.shape, jnp.float32)
    (grad_keys, grad_values), grad_queries = lax.scan(
        block_step, (empty_grad, empty_grad), jnp.arange(block_count, dtype=jnp.int32)
    )
    return (grad_queries.reshape(pack_rows, heads_local, head_dim), grad_keys, grad_values)


def body(
    tokens,
    attn_gain,
    qkv_weight,
    out_weight,
    mlp_gain,
    in_weight,
    down_weight,
    seg_lengths,
    cotangent,
):
    tok_dev, model_width = tokens.shape
    pack_rows = tok_dev * lax.axis_size("tensor")
    heads_local = qkv_weight.shape[1]
    head_dim = qkv_weight.shape[2] // 3
    hidden_local = in_weight.shape[2]
    score_scale = head_dim ** (-0.5)
    query_block = min(512, pack_rows)
    qkv_full, out_full, in_full, down_full = (
        lax.all_gather(qkv_weight, "dp", axis=0, tiled=True),
        lax.all_gather(out_weight, "dp", axis=1, tiled=True),
        lax.all_gather(in_weight, "dp", axis=0, tiled=True),
        lax.all_gather(down_weight, "dp", axis=1, tiled=True),
    )
    qkv_flat = qkv_full.reshape(model_width, heads_local * 3 * head_dim)
    seg_ids, position = segment_info(seg_lengths[0], pack_rows)
    cos_table, sin_table = rotary(position, head_dim)
    row_data = tokens.astype(jnp.float32)
    normed_attn, unit_attn, inverse_attn = layer_norm(row_data, attn_gain)
    attn_input = lax.all_gather(normed_attn.astype(jnp.bfloat16), "tensor", axis=0, tiled=True)
    mixed_proj = dot_plain(attn_input, qkv_flat).reshape(pack_rows, heads_local, 3, head_dim)
    query_rows = turn(mixed_proj[:, :, 0], cos_table, sin_table).astype(jnp.bfloat16)
    key_rows = turn(mixed_proj[:, :, 1], cos_table, sin_table).astype(jnp.bfloat16)
    value_rows = mixed_proj[:, :, 2].astype(jnp.bfloat16)
    attended, log_totals = attention_forward(
        query_rows, key_rows, value_rows, seg_ids, query_block, score_scale
    )
    attended = attended.reshape(pack_rows, heads_local * head_dim).astype(jnp.bfloat16)
    residual = row_data + lax.psum_scatter(
        dot_plain(attended, out_full).astype(jnp.bfloat16),
        "tensor",
        scatter_dimension=0,
        tiled=True,
    ).astype(jnp.float32)
    normed_mlp, unit_mlp, inverse_mlp = layer_norm(residual, mlp_gain)
    mlp_input = normed_mlp.astype(jnp.bfloat16)
    mlp_rows = lax.all_gather(mlp_input, "tensor", axis=0, tiled=True)
    in_flat = in_full.reshape(model_width, -1)
    lifted = dot_plain(mlp_rows, in_flat).reshape(pack_rows, 2, hidden_local)
    act_gelu, act_slope = gelu_parts(lifted[:, 0])
    activated = (act_gelu * lifted[:, 1]).astype(jnp.bfloat16)
    layer_out = (
        residual
        + lax.psum_scatter(
            dot_plain(activated, down_full).astype(jnp.bfloat16),
            "tensor",
            scatter_dimension=0,
            tiled=True,
        ).astype(jnp.float32)
    ).astype(jnp.bfloat16)
    cotangent_rows = lax.all_gather(cotangent, "tensor", axis=0, tiled=True)
    grad_act = dot_last(cotangent_rows, down_full)
    grad_lifted = jnp.concatenate(
        [grad_act * lifted[:, 1] * act_slope, grad_act * act_gelu], axis=1
    ).astype(jnp.bfloat16)
    grad_mlp_in = lax.psum_scatter(
        dot_last(grad_lifted, in_flat).astype(jnp.bfloat16),
        "tensor",
        scatter_dimension=0,
        tiled=True,
    ).astype(jnp.float32)
    grad_in_part = dot_first(mlp_rows, grad_lifted).reshape(in_full.shape)
    grad_down_part = dot_first(activated, cotangent_rows)
    grad_resid_norm, mlp_gain_part = norm_back(grad_mlp_in, unit_mlp, inverse_mlp, mlp_gain)
    grad_residual = cotangent.astype(jnp.float32) + grad_resid_norm
    grad_branch = lax.all_gather(grad_residual.astype(jnp.bfloat16), "tensor", axis=0, tiled=True)
    grad_out_part = dot_first(attended, grad_branch)
    grad_attended = (
        dot_last(grad_branch, out_full)
        .astype(jnp.bfloat16)
        .reshape(pack_rows, heads_local, head_dim)
    )
    grad_queries, grad_keys, grad_values = attention_backward(
        query_rows,
        key_rows,
        value_rows,
        grad_attended,
        log_totals,
        seg_ids,
        query_block,
        score_scale,
    )
    grad_mixed = jnp.stack(
        [
            turn_back(grad_queries, cos_table, sin_table),
            turn_back(grad_keys, cos_table, sin_table),
            grad_values,
        ],
        axis=2,
    )
    grad_mixed = grad_mixed.reshape(pack_rows, heads_local * 3 * head_dim).astype(jnp.bfloat16)
    grad_qkv_part = dot_first(attn_input, grad_mixed).reshape(qkv_full.shape)
    grad_attn_in = lax.psum_scatter(
        dot_last(grad_mixed, qkv_flat).astype(jnp.bfloat16),
        "tensor",
        scatter_dimension=0,
        tiled=True,
    ).astype(jnp.float32)
    grad_rows_attn, attn_gain_part = norm_back(grad_attn_in, unit_attn, inverse_attn, attn_gain)
    grad_tokens = (grad_residual + grad_rows_attn).astype(jnp.bfloat16)
    qkv_grad, out_grad, in_grad, down_grad = (
        lax.psum_scatter(
            grad_qkv_part.astype(jnp.bfloat16), "dp", scatter_dimension=0, tiled=True
        ).astype(jnp.float32),
        lax.psum_scatter(
            grad_out_part.astype(jnp.bfloat16), "dp", scatter_dimension=1, tiled=True
        ).astype(jnp.float32),
        lax.psum_scatter(
            grad_in_part.astype(jnp.bfloat16), "dp", scatter_dimension=0, tiled=True
        ).astype(jnp.float32),
        lax.psum_scatter(
            grad_down_part.astype(jnp.bfloat16), "dp", scatter_dimension=1, tiled=True
        ).astype(jnp.float32),
    )
    attn_gain_grad, mlp_gain_grad = lax.psum((attn_gain_part, mlp_gain_part), ("dp", "tensor"))
    return (
        layer_out,
        grad_tokens,
        attn_gain_grad,
        qkv_grad,
        out_grad,
        mlp_gain_grad,
        in_grad,
        down_grad,
    )


def fast_body(
    tokens,
    attn_gain,
    qkv_weight,
    out_weight,
    mlp_gain,
    in_weight,
    down_weight,
    seg_lengths,
    cotangent,
):
    tok_dev, model_width = tokens.shape
    pack_rows = tok_dev * 4
    heads_local = qkv_weight.shape[1]
    head_dim = qkv_weight.shape[2] // 3
    hidden_local = in_weight.shape[2]
    row_data = tokens.astype(F32)
    normed_attn, unit_attn, inverse_attn = layer_norm(row_data, attn_gain)
    in_full = lax.all_gather(in_weight, "dp", axis=0, tiled=True)
    down_full = lax.all_gather(down_weight, "dp", axis=1, tiled=True)
    attn_input, qkv_flat, out_full = gather_first(
        1,
        normed_attn.astype(BF),
        (qkv_weight.reshape(qkv_weight.shape[0], heads_local * 3 * head_dim), out_weight),
        (0, 1),
    )
    seg_ids, position = segment_info(seg_lengths[0], pack_rows)
    cos_table, sin_table = rotary(position, head_dim)
    ones, zeros = jnp.ones((pack_rows, head_dim), F32), jnp.zeros((pack_rows, head_dim), F32)
    cos_wide = jnp.concatenate([cos_table] * 4 + [ones] + [cos_table] * 4 + [ones], axis=1)
    sin_wide = jnp.concatenate(([-sin_table, sin_table] * 2 + [zeros]) * 2, axis=1)
    seg_col, seg_row = seg_ids[:, None], seg_ids[None, :]
    mixed_proj = dot_plain(attn_input, qkv_flat)
    qkv_rows, attended, log_totals = attend(mixed_proj, cos_wide, sin_wide, seg_col, seg_row)
    residual = row_data + reduce_sums(2, dot_plain(attended, out_full).astype(BF), (), ())[0]
    normed_mlp, unit_mlp, inverse_mlp = layer_norm(residual, mlp_gain)
    mlp_rows, cotangent_rows = gather_rows(3, normed_mlp.astype(BF), cotangent)
    in_flat = in_full.reshape(model_width, -1)
    lifted = dot_plain(mlp_rows, in_flat)
    gate = lifted[:, hidden_local:]
    act_gelu, act_slope = gelu_parts(lifted[:, :hidden_local])
    activated = (act_gelu * gate).astype(BF)
    grad_act = dot_last(cotangent_rows, down_full)
    grad_lifted = jnp.concatenate(
        [grad_act * gate * act_slope, grad_act * act_gelu], axis=1
    ).astype(BF)
    grad_mlp_in = reduce_sums(4, dot_last(grad_lifted, in_flat).astype(BF), (), ())[0]
    layer_sum = lax.psum_scatter(
        dot_plain(activated, down_full).astype(BF), "tensor", scatter_dimension=0, tiled=True
    )
    layer_out = (residual + layer_sum.astype(F32)).astype(BF)
    grad_in_part = dot_first(mlp_rows, grad_lifted).reshape(in_full.shape)
    grad_down_part = dot_first(activated, cotangent_rows)
    in_grad = lax.psum_scatter(
        grad_in_part.astype(BF), "dp", scatter_dimension=0, tiled=True
    ).astype(F32)
    down_grad = lax.psum_scatter(
        grad_down_part.astype(BF), "dp", scatter_dimension=1, tiled=True
    ).astype(F32)
    grad_resid_norm, mlp_gain_part = norm_back(grad_mlp_in, unit_mlp, inverse_mlp, mlp_gain)
    grad_residual = cotangent.astype(F32) + grad_resid_norm
    grad_branch = gather_rows(5, grad_residual.astype(BF))[0]
    grad_out_part = dot_first(attended, grad_branch).astype(BF)
    grad_attended = dot_last(grad_branch, out_full).astype(BF)
    grad_mixed = attend_back(
        qkv_rows, grad_attended, log_totals, cos_wide, sin_wide, seg_col, seg_row
    )
    grad_qkv_part = dot_first(attn_input, grad_mixed).astype(BF)
    grad_attn_in, qkv_grad, out_grad = reduce_sums(
        6, dot_last(grad_mixed, qkv_flat).astype(BF), (grad_qkv_part, grad_out_part), (0, 1)
    )
    grad_rows_attn, attn_gain_part = norm_back(grad_attn_in, unit_attn, inverse_attn, attn_gain)
    grad_tokens = (grad_residual + grad_rows_attn).astype(BF)
    gains = sum_gains(7, jnp.concatenate([attn_gain_part[None], mlp_gain_part[None], jnp.zeros((6, model_width), F32)]))
    return (
        layer_out,
        grad_tokens,
        gains[0],
        qkv_grad.reshape(qkv_weight.shape),
        out_grad,
        gains[1],
        in_grad,
        down_grad,
    )


def solution(mesh):
    fast = mesh.shape["tensor"] == 4 and mesh.shape["dp"] == 8
    chosen = fast_body if fast else body
    in_specs = (
        P(("dp", "tensor"), None),
        P(),
        P("dp", "tensor", None),
        P("tensor", "dp"),
        P(),
        P("dp", None, "tensor"),
        P("tensor", "dp"),
        P("dp", None),
        P(("dp", "tensor"), None),
    )
    out_specs = (
        P(("dp", "tensor"), None),
        P(("dp", "tensor"), None),
        P(),
        P("dp", "tensor", None),
        P("tensor", "dp"),
        P(),
        P("dp", None, "tensor"),
        P("tensor", "dp"),
    )
    return jax.shard_map(chosen, mesh=mesh, in_specs=in_specs, out_specs=out_specs, check_vma=False)
```

```python
import math

import jax
import jax.numpy as jnp
from jax import lax
from jax.experimental import pallas as pl
from jax.experimental.pallas import tpu as pltpu
from jax.sharding import PartitionSpec as P

NORM_EPS = 1e-05
ROPE_BASE = 160000.0
HALF_ROOT = 0.7071067811865476
INV_ROOT_TAU = 0.3989422804014327
MASKED_SCORE = -1e30


def dot_plain(left, right):
    return jnp.dot(left, right, preferred_element_type=jnp.float32)


def dot_first(left, right):
    return lax.dot_general(
        left, right, (((0,), (0,)), ((), ())), preferred_element_type=jnp.float32
    )


def dot_last(left, right):
    return lax.dot_general(
        left, right, (((1,), (1,)), ((), ())), preferred_element_type=jnp.float32
    )


MESH_ID = pl.DeviceIdType.MESH
VM = pltpu.VMEM
BF = jnp.bfloat16
F32 = jnp.float32
DMA = pltpu.SemaphoreType.DMA
SPLIT = 4


def swap_halves(wide):
    width = wide.shape[1]
    lane = lax.broadcasted_iota(jnp.int32, wide.shape, 1) % 64
    return jnp.where(lane < 32, pltpu.roll(wide, width - 32, 1), pltpu.roll(wide, 32, 1))


def wide_tables(cos_ref, sin_ref):
    cos_two, sin_two = cos_ref[...], sin_ref[...]
    ones, zeros = jnp.ones_like(cos_two), jnp.zeros_like(sin_two)
    return (
        jnp.concatenate([cos_two, cos_two, ones] * 2, axis=1),
        jnp.concatenate([sin_two, sin_two, zeros] * 2, axis=1),
    )


def attend_kernel(mixed_ref, cos_ref, sin_ref, segc_ref, segr_ref, qkv_ref, att_ref, lse_ref):
    mixed = mixed_ref[...]
    cos_wide, sin_wide = wide_tables(cos_ref, sin_ref)
    qkv_ref[...] = (mixed * cos_wide + swap_halves(mixed) * sin_wide).astype(BF)
    rows = mixed_ref.shape[0]
    block = 256
    values_t = [
        qkv_ref[:, h * 192 + 128 : h * 192 + 192].astype(F32).T.astype(BF) for h in range(2)
    ]

    def step(i, carry):
        start = pl.multiple_of(i * block, block)
        same = segc_ref[...] == segr_ref[:, pl.ds(start, block)]
        for head in range(2):
            base = head * 192
            query = qkv_ref[pl.ds(start, block), base : base + 64] * BF(0.125)
            scores = dot_last(qkv_ref[:, base + 64 : base + 128], query)
            scores = jnp.where(same, scores, MASKED_SCORE)
            top = jnp.max(scores, axis=0, keepdims=True)
            expo = jnp.exp(scores - top)
            total = jnp.sum(expo, axis=0, keepdims=True)
            weights = (expo * (1.0 / total)).astype(BF)
            out_t = dot_plain(values_t[head], weights)
            att_ref[pl.ds(start, block), head * 64 : head * 64 + 64] = out_t.T.astype(BF)
            lse_ref[0, head : head + 1, pl.ds(start, block)] = top + jnp.log(total)
        return carry

    lax.fori_loop(0, rows // block, step, 0)


def attend_back_kernel(qkv_ref, ga_ref, lse_ref, cos_ref, sin_ref, segc_ref, segr_ref, gm_ref, acc):
    rows = qkv_ref.shape[0]
    block = 256
    keys_t = [
        qkv_ref[:, h * 192 + 64 : h * 192 + 128].astype(F32).T.astype(BF) for h in range(2)
    ]

    def step(i, carry):
        start = pl.multiple_of(i * block, block)
        same = segc_ref[...] == segr_ref[:, pl.ds(start, block)]
        sums = []
        for head in range(2):
            base = head * 192
            query = qkv_ref[pl.ds(start, block), base : base + 64] * BF(0.125)
            grad_o = ga_ref[pl.ds(start, block), head * 64 : head * 64 + 64]
            scores = dot_last(qkv_ref[:, base + 64 : base + 128], query)
            scores = jnp.where(same, scores, MASKED_SCORE)
            probs = jnp.exp(scores - lse_ref[0, head : head + 1, pl.ds(start, block)])
            grad_p = dot_last(qkv_ref[:, base + 128 : base + 192], grad_o)
            inner = jnp.sum(probs * grad_p, axis=0, keepdims=True)
            grad_s = (probs * (grad_p - inner)).astype(BF)
            sums.append(carry[2 * head] + dot_plain(grad_s, query))
            sums.append(carry[2 * head + 1] + dot_plain(probs.astype(BF), grad_o))
            grad_q = dot_plain(keys_t[head], grad_s) * 0.125
            acc[pl.ds(start, block), base : base + 64] = grad_q.T
        return tuple(sums)

    empty = jnp.zeros((rows, 64), F32)
    sums = lax.fori_loop(0, rows // block, step, (empty,) * 4)
    for head in range(2):
        base = head * 192
        acc[:, base + 64 : base + 128] = sums[2 * head]
        acc[:, base + 128 : base + 192] = sums[2 * head + 1]
    grads = acc[...]
    cos_wide, sin_wide = wide_tables(cos_ref, sin_ref)
    gm_ref[...] = (grads * cos_wide - swap_halves(grads) * sin_wide).astype(BF)


def attend(mixed, cos_wide, sin_wide, seg_col, seg_row):
    rows, cols = mixed.shape
    pairs = cols // 384
    whole = lambda p: (0, 0)
    return pl.pallas_call(
        attend_kernel,
        grid=(pairs,),
        in_specs=[
            pl.BlockSpec((rows, 384), lambda p: (0, p)),
            pl.BlockSpec((rows, 64), whole),
            pl.BlockSpec((rows, 64), whole),
            pl.BlockSpec((rows, 1), whole),
            pl.BlockSpec((1, rows), whole),
        ],
        out_specs=[
            pl.BlockSpec((rows, 384), lambda p: (0, p)),
            pl.BlockSpec((rows, 128), lambda p: (0, p)),
            pl.BlockSpec((1, 2, rows), lambda p: (p, 0, 0)),
        ],
        out_shape=[
            jax.ShapeDtypeStruct((rows, cols), BF),
            jax.ShapeDtypeStruct((rows, pairs * 128), BF),
            jax.ShapeDtypeStruct((pairs, 2, rows), F32),
        ],
        cost_estimate=pl.CostEstimate(
            flops=pairs * 2 * rows * rows * 64 * 4,
            transcendentals=pairs * 2 * rows * rows,
            bytes_accessed=rows * cols * 8,
        ),
        compiler_params=pltpu.CompilerParams(vmem_limit_bytes=48 << 20),
        name="attend",
    )(mixed, cos_wide, sin_wide, seg_col, seg_row)


def attend_back(qkv, grad_att, lse, cos_wide, sin_wide, seg_col, seg_row):
    rows, cols = qkv.shape
    pairs = cols // 384
    whole = lambda p: (0, 0)
    return pl.pallas_call(
        attend_back_kernel,
        grid=(pairs,),
        in_specs=[
            pl.BlockSpec((rows, 384), lambda p: (0, p)),
            pl.BlockSpec((rows, 128), lambda p: (0, p)),
            pl.BlockSpec((1, 2, rows), lambda p: (p, 0, 0)),
            pl.BlockSpec((rows, 64), whole),
            pl.BlockSpec((rows, 64), whole),
            pl.BlockSpec((rows, 1), whole),
            pl.BlockSpec((1, rows), whole),
        ],
        out_specs=pl.BlockSpec((rows, 384), lambda p: (0, p)),
        out_shape=jax.ShapeDtypeStruct((rows, cols), BF),
        scratch_shapes=[VM((rows, 384), F32)],
        cost_estimate=pl.CostEstimate(
            flops=pairs * 2 * rows * rows * 64 * 10,
            transcendentals=pairs * 2 * rows * rows,
            bytes_accessed=rows * cols * 8,
        ),
        compiler_params=pltpu.CompilerParams(vmem_limit_bytes=48 << 20),
        name="attend_back",
    )(qkv, grad_att, lse, cos_wide, sin_wide, seg_col, seg_row)


def remote(source, target, send_sem, recv_sem, device):
    return pltpu.make_async_remote_copy(
        src_ref=source, dst_ref=target, send_sem=send_sem, recv_sem=recv_sem,
        device_id=device, device_id_type=MESH_ID,
    )


def greet(peers):
    barrier = pltpu.get_barrier_semaphore()
    for peer in peers:
        pl.semaphore_signal(barrier, inc=1, device_id=peer, device_id_type=MESH_ID)
    pl.semaphore_wait(barrier, len(peers))


def near_peers():
    dp, mine = lax.axis_index("dp"), lax.axis_index("tensor")
    across = (mine + 2) % 4
    beside = mine + 1 - 2 * (mine % 2)
    return dp, mine, across, beside


def far_peers():
    dp, mine = lax.axis_index("dp"), lax.axis_index("tensor")
    level, side = dp // 2, dp % 2
    cross = dp + 1 - 2 * side
    ahead = [((level + k) % 4) * 2 + side for k in range(4)]
    behind = [((level + 4 - k) % 4) * 2 + side for k in range(4)]
    return dp, mine, cross, ahead, behind


class RowGather:
    sems = [DMA((SPLIT,)), DMA((SPLIT,)), DMA((SPLIT + 1,)), DMA((SPLIT + 1,)), DMA]

    def __init__(self, source, target, sems):
        self.source, self.target, self.sems_in = source, target, sems
        self.rows = source.shape[0]

    def start(self):
        dp, mine, across, beside = near_peers()
        send_y, recv_y, send_c, recv_c, own = self.sems_in
        rows, part = self.rows, self.rows // SPLIT
        self.links = []
        for j in range(SPLIT):
            link = remote(
                self.source.at[pl.ds(j * part, part)],
                self.target.at[pl.ds(mine * rows + j * part, part)],
                send_y.at[j], recv_y.at[j], (dp, across))
            link.start()
            self.links.append(link)
        self.beside = remote(
            self.source, self.target.at[pl.ds(mine * rows, rows)],
            send_c.at[SPLIT], recv_c.at[SPLIT], (dp, beside))
        self.beside.start()
        self.local = pltpu.make_async_copy(
            self.source, self.target.at[pl.ds(mine * rows, rows)], own)
        self.local.start()
        self.forwards = []

    def step(self, j):
        dp, mine, across, beside = near_peers()
        send_y, recv_y, send_c, recv_c, own = self.sems_in
        rows, part = self.rows, self.rows // SPLIT
        place = self.target.at[pl.ds(across * rows + j * part, part)]
        remote(self.source.at[pl.ds(j * part, part)], place,
               send_y.at[j], recv_y.at[j], (dp, across)).wait_recv()
        forward = remote(place, place, send_c.at[j], recv_c.at[j], (dp, beside))
        forward.start()
        self.forwards.append(forward)

    def finish(self):
        dp, mine, across, beside = near_peers()
        send_y, recv_y, send_c, recv_c, own = self.sems_in
        rows, part = self.rows, self.rows // SPLIT
        other = beside
        remote(self.source, self.target.at[pl.ds(other * rows, rows)],
               send_c.at[SPLIT], recv_c.at[SPLIT], (dp, beside)).wait_recv()
        diagonal = (beside + 2) % 4
        for j in range(SPLIT):
            place = self.target.at[pl.ds(diagonal * rows + j * part, part)]
            remote(place, place, send_c.at[j], recv_c.at[j], (dp, beside)).wait_recv()
        for link in self.links + self.forwards + [self.beside]:
            link.wait_send()
        self.local.wait()


class WeightGather:
    sems = [DMA((8,)), DMA((8,)), DMA]

    def __init__(self, source, target, sems, axis):
        self.source, self.target, self.sems_in, self.axis = source, target, sems, axis

    def place(self, index):
        size = self.source.shape[self.axis]
        window = pl.ds(pl.multiple_of(index * size, size), size)
        return self.target.at[window] if self.axis == 0 else self.target.at[:, window]

    def start(self):
        dp, mine, cross, ahead, behind = far_peers()
        send, recv, own = self.sems_in
        self.links = []
        for k in (2, 1, 3):
            link = remote(self.source, self.place(dp), send.at[k], recv.at[k], (ahead[k], mine))
            link.start()
            self.links.append(link)
        link = remote(self.source, self.place(dp), send.at[4], recv.at[4], (cross, mine))
        link.start()
        self.links.append(link)
        self.local = pltpu.make_async_copy(self.source, self.place(dp), own)
        self.local.start()

    def step(self, k):
        dp, mine, cross, ahead, behind = far_peers()
        send, recv, own = self.sems_in
        place = self.place(behind[k])
        remote(self.source, place, send.at[k], recv.at[k], (ahead[k], mine)).wait_recv()
        link = remote(place, place, send.at[4 + k], recv.at[4 + k], (cross, mine))
        link.start()
        self.links.append(link)

    def finish(self):
        dp, mine, cross, ahead, behind = far_peers()
        send, recv, own = self.sems_in
        for k in range(4):
            index = behind[k] + 1 - 2 * (dp % 2)
            place = self.place(index)
            remote(place, place, send.at[4 + k], recv.at[4 + k], (cross, mine)).wait_recv()
        for link in self.links:
            link.wait_send()
        self.local.wait()


class RowReduce:
    sems = [DMA((SPLIT + 1,)), DMA((SPLIT + 1,)), DMA((SPLIT,)), DMA((SPLIT,))]

    @staticmethod
    def scratch(rows, width):
        return [VM((rows, width), BF), VM((rows, width), BF), VM((rows, width), BF), VM((rows, width), BF)]

    def __init__(self, source, target, scratch, sems):
        self.source, self.target, self.scratch_in, self.sems_in = source, target, scratch, sems
        self.rows = target.shape[0]

    def start(self):
        dp, mine, across, beside = near_peers()
        send_c, recv_c, send_y, recv_y = self.sems_in
        far_in, near_in, sums, y_in = self.scratch_in
        rows, part = self.rows, self.rows // SPLIT
        diagonal = (beside + 2) % 4
        self.links = []
        for j in range(SPLIT):
            link = remote(
                self.source.at[pl.ds(diagonal * rows + j * part, part)],
                far_in.at[pl.ds(j * part, part)], send_c.at[j], recv_c.at[j], (dp, beside))
            link.start()
            self.links.append(link)
        link = remote(
            self.source.at[pl.ds(beside * rows, rows)], near_in,
            send_c.at[SPLIT], recv_c.at[SPLIT], (dp, beside))
        link.start()
        self.links.append(link)

    def step(self, j):
        dp, mine, across, beside = near_peers()
        send_c, recv_c, send_y, recv_y = self.sems_in
        far_in, near_in, sums, y_in = self.scratch_in
        rows, part = self.rows, self.rows // SPLIT
        window = pl.ds(j * part, part)
        self.links[j].wait_recv()
        sums[window] = (
            self.source[pl.ds(across * rows + j * part, part)].astype(F32)
            + far_in[window].astype(F32)
        ).astype(BF)
        link = remote(sums.at[window], y_in.at[window], send_y.at[j], recv_y.at[j], (dp, across))
        link.start()
        self.links.append(link)

    def finish(self):
        dp, mine, across, beside = near_peers()
        far_in, near_in, sums, y_in = self.scratch_in
        rows, part = self.rows, self.rows // SPLIT
        self.links[SPLIT].wait_recv()
        for j in range(SPLIT):
            window = pl.ds(j * part, part)
            self.links[SPLIT + 1 + j].wait_recv()
            self.target[window] = (
                self.source[pl.ds(mine * rows + j * part, part)].astype(F32)
                + near_in[window].astype(F32)
                + y_in[window].astype(F32)
            )
        for link in self.links:
            link.wait_send()


class WeightReduce:
    sems = [DMA((8,)), DMA((8,))]

    @staticmethod
    def scratch(shape):
        return [VM((4, *shape), BF), VM((4, *shape), BF), VM((4, *shape), BF)]

    def __init__(self, source, target, scratch, sems, axis):
        self.source, self.target, self.scratch_in, self.sems_in = source, target, scratch, sems
        self.axis = axis

    def window(self, index):
        size = self.target.shape[self.axis]
        window = pl.ds(pl.multiple_of(index * size, size), size)
        return (window,) if self.axis == 0 else (slice(None), window)

    def start(self):
        dp, mine, cross, ahead, behind = far_peers()
        send, recv = self.sems_in
        x_in, sums, z_in = self.scratch_in
        self.links = {}
        for k in (2, 1, 3, 0):
            index = ahead[k] + 1 - 2 * (dp % 2)
            link = remote(self.source.at[self.window(index)], x_in.at[k],
                          send.at[k], recv.at[k], (cross, mine))
            link.start()
            self.links[k] = link

    def step(self, k):
        dp, mine, cross, ahead, behind = far_peers()
        send, recv = self.sems_in
        x_in, sums, z_in = self.scratch_in
        self.links[k].wait_recv()
        sums[k] = (self.source[self.window(ahead[k])].astype(F32) + x_in[k].astype(F32)).astype(BF)
        if k:
            link = remote(sums.at[k], z_in.at[k], send.at[4 + k], recv.at[4 + k], (ahead[k], mine))
            link.start()
            self.links[4 + k] = link

    def finish(self):
        x_in, sums, z_in = self.scratch_in
        for k in (1, 2, 3):
            self.links[4 + k].wait_recv()
        self.target[...] = (
            sums[0].astype(F32) + z_in[1].astype(F32) + z_in[2].astype(F32) + z_in[3].astype(F32)
        )
        for link in self.links.values():
            link.wait_send()


def run_parts(near, far):
    dp, mine, across, beside = near_peers()
    peers = [(dp, across), (dp, beside)] if near else []
    if far:
        dp, mine, cross, ahead, behind = far_peers()
        peers += [(cross, mine)] + [(ahead[k], mine) for k in (1, 2, 3)]
    greet(peers)
    for part in near + far:
        part.start()
    for j in range(SPLIT):
        for part in near:
            part.step(j)
        for part in far:
            k = (2, 1, 3, 0)[j]
            if k or isinstance(part, WeightReduce):
                part.step(k)
    for part in near + far:
        part.finish()


def comm_call(kernel, args, outs, out_spaces, scratch, ident, name):
    return pl.pallas_call(
        kernel,
        out_shape=[jax.ShapeDtypeStruct(*out) for out in outs],
        in_specs=[pl.BlockSpec(memory_space=VM)] * len(args),
        out_specs=[pl.BlockSpec(memory_space=space) for space in out_spaces],
        scratch_shapes=scratch,
        compiler_params=pltpu.CompilerParams(
            collective_id=ident, has_side_effects=True, vmem_limit_bytes=40 << 20
        ),
        name=name,
    )(*args)


def gather_parts(ident, rows, weights=(), axes=()):
    near_count, count = len(rows), len(rows) + len(weights)
    per_row, per_weight = len(RowGather.sems), len(WeightGather.sems)

    def kernel(*refs):
        ins, outs, sems = refs[:count], refs[count : 2 * count], refs[2 * count :]
        near = [
            RowGather(ins[i], outs[i], sems[i * per_row : (i + 1) * per_row])
            for i in range(near_count)
        ]
        sems = sems[near_count * per_row :]
        far = [
            WeightGather(
                ins[near_count + i], outs[near_count + i],
                sems[i * per_weight : (i + 1) * per_weight], axes[i])
            for i in range(len(weights))
        ]
        run_parts(near, far)

    shapes = [((4 * a.shape[0], a.shape[1]), BF) for a in rows]
    for weight, axis in zip(weights, axes):
        shape = list(weight.shape)
        shape[axis] = shape[axis] * 8
        shapes.append((tuple(shape), BF))
    return comm_call(
        kernel, (*rows, *weights), shapes, [pl.ANY] * count,
        RowGather.sems * near_count + WeightGather.sems * len(weights), ident, "gather_parts")


def reduce_sums(ident, partials, grads=(), axes=()):
    near_count, count = len(partials), len(partials) + len(grads)
    shapes, scratch = [], []
    for partial in partials:
        shape = (partial.shape[0] // 4, partial.shape[1])
        shapes.append((shape, F32))
        scratch = scratch + RowReduce.scratch(*shape) + RowReduce.sems
    for grad, axis in zip(grads, axes):
        shape = list(grad.shape)
        shape[axis] = shape[axis] // 8
        shapes.append((tuple(shape), F32))
        scratch = scratch + WeightReduce.scratch(tuple(shape)) + WeightReduce.sems

    def kernel(*refs):
        ins, outs, rest = refs[:count], refs[count : 2 * count], refs[2 * count :]
        near = []
        for i in range(near_count):
            near.append(RowReduce(ins[i], outs[i], rest[:4], rest[4:8]))
            rest = rest[8:]
        far = []
        for i in range(len(grads)):
            far.append(WeightReduce(ins[near_count + i], outs[near_count + i], rest[:3], rest[3:5], axes[i]))
            rest = rest[5:]
        run_parts(near, far)

    return comm_call(kernel, (*partials, *grads), shapes, [VM] * count, scratch, ident, "reduce_sums")


def sum_gains_kernel(part_ref, out_ref, near_in, mid, far_in, send_n, recv_n, send_f, recv_f):
    dp, mine = lax.axis_index("dp"), lax.axis_index("tensor")
    near = [(dp, (mine + k) % 4) for k in range(1, 4)]
    far = [((dp + k) % 8, mine) for k in range(1, 8)]
    greet(near + far)
    links = []
    for k in range(3):
        link = remote(part_ref, near_in.at[k], send_n.at[k], recv_n.at[k], near[k])
        link.start()
        links.append(link)
    for link in links:
        link.wait_recv()
    mid[...] = part_ref[...] + near_in[0] + near_in[1] + near_in[2]
    more = []
    for k in range(7):
        link = remote(mid, far_in.at[k], send_f.at[k], recv_f.at[k], far[k])
        link.start()
        more.append(link)
    total = mid[...]
    for k in range(7):
        more[k].wait_recv()
        total = total + far_in[k]
    out_ref[...] = total
    for link in links + more:
        link.wait_send()


def sum_gains(ident, parts):
    shape = parts.shape
    return comm_call(
        sum_gains_kernel, (parts,), [(shape, F32)], [VM],
        [VM((3, *shape), F32), VM(shape, F32), VM((7, *shape), F32),
         DMA((3,)), DMA((3,)), DMA((7,)), DMA((7,))], ident, "sum_gains")[0]


def layer_norm(row_data, norm_gain):
    centered = row_data - jnp.mean(row_data, axis=-1, keepdims=True)
    inverse = lax.rsqrt(jnp.mean(centered * centered, axis=-1, keepdims=True) + NORM_EPS)
    unit_rows = centered * inverse
    return (unit_rows * norm_gain, unit_rows, inverse)


def norm_back(grad_normed, unit_rows, inverse, norm_gain):
    scaled = grad_normed * norm_gain
    grad_rows = inverse * (
        scaled
        - jnp.mean(scaled, axis=-1, keepdims=True)
        - unit_rows * jnp.mean(scaled * unit_rows, axis=-1, keepdims=True)
    )
    return (grad_rows, jnp.sum(grad_normed * unit_rows, axis=0))


def gelu_parts(value_in):
    normal_cdf = 0.5 * (1.0 + lax.erf(value_in * HALF_ROOT))
    slope = normal_cdf + value_in * INV_ROOT_TAU * jnp.exp(-0.5 * value_in * value_in)
    return (value_in * normal_cdf, slope)


def segment_info(seg_lens, pack_rows):
    seg_ends = jnp.cumsum(seg_lens)
    places = lax.iota(jnp.int32, pack_rows)
    before = seg_ends[None, :] <= places[:, None]
    seg_ids = jnp.sum(before.astype(jnp.int32), axis=1)
    seg_first = jnp.sum(jnp.where(before, seg_lens[None, :], 0), axis=1)
    return (seg_ids, places - seg_first)


def rotary(position, head_dim):
    half_dim = head_dim // 2
    inv_freq = jnp.exp(lax.iota(jnp.float32, half_dim) * (-2.0 * math.log(ROPE_BASE) / head_dim))
    angles = position.astype(jnp.float32)[:, None] * inv_freq[None, :]
    return (jnp.cos(angles), jnp.sin(angles))


def turn(vectors, cos_table, sin_table):
    half_dim = vectors.shape[-1] // 2
    front_half = vectors[..., :half_dim]
    back_half = vectors[..., half_dim:]
    cos_part = cos_table[:, None, :]
    sin_part = sin_table[:, None, :]
    return jnp.concatenate(
        [
            front_half * cos_part - back_half * sin_part,
            back_half * cos_part + front_half * sin_part,
        ],
        axis=-1,
    )


def turn_back(grads_in, cos_table, sin_table):
    half_dim = grads_in.shape[-1] // 2
    front_half = grads_in[..., :half_dim]
    back_half = grads_in[..., half_dim:]
    cos_part = cos_table[:, None, :]
    sin_part = sin_table[:, None, :]
    return jnp.concatenate(
        [
            front_half * cos_part + back_half * sin_part,
            back_half * cos_part - front_half * sin_part,
        ],
        axis=-1,
    )


def block_scores(query_part, key_part, seg_query, seg_key, score_scale):
    scores = (
        jnp.einsum("qhd,khd->hqk", query_part, key_part, preferred_element_type=jnp.float32)
        * score_scale
    )
    return jnp.where((seg_query[:, None] == seg_key[None, :])[None], scores, MASKED_SCORE)


def attention_forward(query_rows, key_rows, value_rows, seg_ids, query_block, score_scale):
    pack_rows, heads_local, head_dim = query_rows.shape
    block_count = pack_rows // query_block

    def one_block(block_index):
        query_start = block_index * query_block
        query_part = lax.dynamic_slice_in_dim(query_rows, query_start, query_block, 0)
        seg_query = lax.dynamic_slice_in_dim(seg_ids, query_start, query_block, 0)
        scores = block_scores(query_part, key_rows, seg_query, seg_ids, score_scale)
        row_top = jnp.max(scores, axis=-1, keepdims=True)
        expo = jnp.exp(scores - row_top)
        row_total = jnp.sum(expo, axis=-1, keepdims=True)
        weights = (expo / row_total).astype(jnp.bfloat16)
        result = jnp.einsum("hqk,khd->qhd", weights, value_rows, preferred_element_type=jnp.float32)
        return (result, (row_top + jnp.log(row_total))[..., 0])

    results, log_totals = lax.map(one_block, jnp.arange(block_count, dtype=jnp.int32))
    return (results.reshape(pack_rows, heads_local, head_dim), log_totals)


def attention_backward(
    query_rows, key_rows, value_rows, grad_attended, log_totals, seg_ids, query_block, score_scale
):
    pack_rows, heads_local, head_dim = query_rows.shape
    block_count = pack_rows // query_block

    def block_step(running, block_index):
        grad_keys, grad_values = running
        query_start = block_index * query_block
        query_part = lax.dynamic_slice_in_dim(query_rows, query_start, query_block, 0)
        grad_part = lax.dynamic_slice_in_dim(grad_attended, query_start, query_block, 0)
        seg_query = lax.dynamic_slice_in_dim(seg_ids, query_start, query_block, 0)
        scores = block_scores(query_part, key_rows, seg_query, seg_ids, score_scale)
        probs = jnp.exp(scores - log_totals[block_index][..., None])
        grad_probs = jnp.einsum(
            "qhd,khd->hqk", grad_part, value_rows, preferred_element_type=jnp.float32
        )
        inner = jnp.sum(probs * grad_probs, axis=-1, keepdims=True)
        grad_scores = (probs * (grad_probs - inner)).astype(jnp.bfloat16) * score_scale
        grad_query_part = jnp.einsum(
            "hqk,khd->qhd", grad_scores, key_rows, preferred_element_type=jnp.float32
        )
        grad_key_part = jnp.einsum(
            "hqk,qhd->khd", grad_scores, query_part, preferred_element_type=jnp.float32
        )
        grad_value_part = jnp.einsum(
            "hqk,qhd->khd",
            probs.astype(jnp.bfloat16),
            grad_part,
            preferred_element_type=jnp.float32,
        )
        grad_keys = grad_keys + grad_key_part
        grad_values = grad_values + grad_value_part
        return ((grad_keys, grad_values), grad_query_part)

    empty_grad = jnp.zeros(query_rows.shape, jnp.float32)
    (grad_keys, grad_values), grad_queries = lax.scan(
        block_step, (empty_grad, empty_grad), jnp.arange(block_count, dtype=jnp.int32)
    )
    return (grad_queries.reshape(pack_rows, heads_local, head_dim), grad_keys, grad_values)


def body(
    tokens,
    attn_gain,
    qkv_weight,
    out_weight,
    mlp_gain,
    in_weight,
    down_weight,
    seg_lengths,
    cotangent,
):
    tok_dev, model_width = tokens.shape
    pack_rows = tok_dev * lax.axis_size("tensor")
    heads_local = qkv_weight.shape[1]
    head_dim = qkv_weight.shape[2] // 3
    hidden_local = in_weight.shape[2]
    score_scale = head_dim ** (-0.5)
    query_block = min(512, pack_rows)
    qkv_full, out_full, in_full, down_full = (
        lax.all_gather(qkv_weight, "dp", axis=0, tiled=True),
        lax.all_gather(out_weight, "dp", axis=1, tiled=True),
        lax.all_gather(in_weight, "dp", axis=0, tiled=True),
        lax.all_gather(down_weight, "dp", axis=1, tiled=True),
    )
    qkv_flat = qkv_full.reshape(model_width, heads_local * 3 * head_dim)
    seg_ids, position = segment_info(seg_lengths[0], pack_rows)
    cos_table, sin_table = rotary(position, head_dim)
    row_data = tokens.astype(jnp.float32)
    normed_attn, unit_attn, inverse_attn = layer_norm(row_data, attn_gain)
    attn_input = lax.all_gather(normed_attn.astype(jnp.bfloat16), "tensor", axis=0, tiled=True)
    mixed_proj = dot_plain(attn_input, qkv_flat).reshape(pack_rows, heads_local, 3, head_dim)
    query_rows = turn(mixed_proj[:, :, 0], cos_table, sin_table).astype(jnp.bfloat16)
    key_rows = turn(mixed_proj[:, :, 1], cos_table, sin_table).astype(jnp.bfloat16)
    value_rows = mixed_proj[:, :, 2].astype(jnp.bfloat16)
    attended, log_totals = attention_forward(
        query_rows, key_rows, value_rows, seg_ids, query_block, score_scale
    )
    attended = attended.reshape(pack_rows, heads_local * head_dim).astype(jnp.bfloat16)
    residual = row_data + lax.psum_scatter(
        dot_plain(attended, out_full).astype(jnp.bfloat16),
        "tensor",
        scatter_dimension=0,
        tiled=True,
    ).astype(jnp.float32)
    normed_mlp, unit_mlp, inverse_mlp = layer_norm(residual, mlp_gain)
    mlp_input = normed_mlp.astype(jnp.bfloat16)
    mlp_rows = lax.all_gather(mlp_input, "tensor", axis=0, tiled=True)
    in_flat = in_full.reshape(model_width, -1)
    lifted = dot_plain(mlp_rows, in_flat).reshape(pack_rows, 2, hidden_local)
    act_gelu, act_slope = gelu_parts(lifted[:, 0])
    activated = (act_gelu * lifted[:, 1]).astype(jnp.bfloat16)
    layer_out = (
        residual
        + lax.psum_scatter(
            dot_plain(activated, down_full).astype(jnp.bfloat16),
            "tensor",
            scatter_dimension=0,
            tiled=True,
        ).astype(jnp.float32)
    ).astype(jnp.bfloat16)
    cotangent_rows = lax.all_gather(cotangent, "tensor", axis=0, tiled=True)
    grad_act = dot_last(cotangent_rows, down_full)
    grad_lifted = jnp.concatenate(
        [grad_act * lifted[:, 1] * act_slope, grad_act * act_gelu], axis=1
    ).astype(jnp.bfloat16)
    grad_mlp_in = lax.psum_scatter(
        dot_last(grad_lifted, in_flat).astype(jnp.bfloat16),
        "tensor",
        scatter_dimension=0,
        tiled=True,
    ).astype(jnp.float32)
    grad_in_part = dot_first(mlp_rows, grad_lifted).reshape(in_full.shape)
    grad_down_part = dot_first(activated, cotangent_rows)
    grad_resid_norm, mlp_gain_part = norm_back(grad_mlp_in, unit_mlp, inverse_mlp, mlp_gain)
    grad_residual = cotangent.astype(jnp.float32) + grad_resid_norm
    grad_branch = lax.all_gather(grad_residual.astype(jnp.bfloat16), "tensor", axis=0, tiled=True)
    grad_out_part = dot_first(attended, grad_branch)
    grad_attended = (
        dot_last(grad_branch, out_full)
        .astype(jnp.bfloat16)
        .reshape(pack_rows, heads_local, head_dim)
    )
    grad_queries, grad_keys, grad_values = attention_backward(
        query_rows,
        key_rows,
        value_rows,
        grad_attended,
        log_totals,
        seg_ids,
        query_block,
        score_scale,
    )
    grad_mixed = jnp.stack(
        [
            turn_back(grad_queries, cos_table, sin_table),
            turn_back(grad_keys, cos_table, sin_table),
            grad_values,
        ],
        axis=2,
    )
    grad_mixed = grad_mixed.reshape(pack_rows, heads_local * 3 * head_dim).astype(jnp.bfloat16)
    grad_qkv_part = dot_first(attn_input, grad_mixed).reshape(qkv_full.shape)
    grad_attn_in = lax.psum_scatter(
        dot_last(grad_mixed, qkv_flat).astype(jnp.bfloat16),
        "tensor",
        scatter_dimension=0,
        tiled=True,
    ).astype(jnp.float32)
    grad_rows_attn, attn_gain_part = norm_back(grad_attn_in, unit_attn, inverse_attn, attn_gain)
    grad_tokens = (grad_residual + grad_rows_attn).astype(jnp.bfloat16)
    qkv_grad, out_grad, in_grad, down_grad = (
        lax.psum_scatter(
            grad_qkv_part.astype(jnp.bfloat16), "dp", scatter_dimension=0, tiled=True
        ).astype(jnp.float32),
        lax.psum_scatter(
            grad_out_part.astype(jnp.bfloat16), "dp", scatter_dimension=1, tiled=True
        ).astype(jnp.float32),
        lax.psum_scatter(
            grad_in_part.astype(jnp.bfloat16), "dp", scatter_dimension=0, tiled=True
        ).astype(jnp.float32),
        lax.psum_scatter(
            grad_down_part.astype(jnp.bfloat16), "dp", scatter_dimension=1, tiled=True
        ).astype(jnp.float32),
    )
    attn_gain_grad, mlp_gain_grad = lax.psum((attn_gain_part, mlp_gain_part), ("dp", "tensor"))
    return (
        layer_out,
        grad_tokens,
        attn_gain_grad,
        qkv_grad,
        out_grad,
        mlp_gain_grad,
        in_grad,
        down_grad,
    )


def fast_body(
    tokens,
    attn_gain,
    qkv_weight,
    out_weight,
    mlp_gain,
    in_weight,
    down_weight,
    seg_lengths,
    cotangent,
):
    tok_dev, model_width = tokens.shape
    pack_rows = tok_dev * 4
    heads_local = qkv_weight.shape[1]
    head_dim = qkv_weight.shape[2] // 3
    hidden_local = in_weight.shape[2]
    row_data = tokens.astype(F32)
    normed_attn, unit_attn, inverse_attn = layer_norm(row_data, attn_gain)
    attn_input, cotangent_rows, qkv_flat, out_full = gather_parts(
        1,
        (normed_attn.astype(BF), cotangent),
        (qkv_weight.reshape(qkv_weight.shape[0], heads_local * 3 * head_dim), out_weight),
        (0, 1),
    )
    in_shard = in_weight.reshape(in_weight.shape[0], 2 * hidden_local)
    in_shard, attn_input = lax.optimization_barrier((in_shard, attn_input))
    in_flat = lax.all_gather(in_shard, "dp", axis=0, tiled=True)
    seg_ids, position = segment_info(seg_lengths[0], pack_rows)
    cos_table, sin_table = rotary(position, head_dim)
    cos_two = jnp.concatenate([cos_table, cos_table], axis=1)
    sin_two = jnp.concatenate([-sin_table, sin_table], axis=1)
    seg_col, seg_row = seg_ids[:, None], seg_ids[None, :]
    mixed_proj = dot_plain(attn_input, qkv_flat)
    qkv_rows, attended, log_totals = attend(mixed_proj, cos_two, sin_two, seg_col, seg_row)
    residual = row_data + reduce_sums(2, (dot_plain(attended, out_full).astype(BF),))[0]
    normed_mlp, unit_mlp, inverse_mlp = layer_norm(residual, mlp_gain)
    mlp_rows, down_full = gather_parts(3, (normed_mlp.astype(BF),), (down_weight,), (1,))
    lifted = dot_plain(mlp_rows, in_flat)
    gate = lifted[:, hidden_local:]
    act_gelu, act_slope = gelu_parts(lifted[:, :hidden_local])
    activated = (act_gelu * gate).astype(BF)
    grad_act = dot_last(cotangent_rows, down_full)
    grad_lifted = jnp.concatenate(
        [grad_act * gate * act_slope, grad_act * act_gelu], axis=1
    ).astype(BF)
    in_grad = lax.psum_scatter(
        dot_first(mlp_rows, grad_lifted).astype(BF), "dp", scatter_dimension=0, tiled=True
    )
    in_grad = in_grad.reshape(in_weight.shape).astype(F32)
    grad_mlp_in, down_grad = reduce_sums(
        4,
        (dot_last(grad_lifted, in_flat).astype(BF),),
        (dot_first(activated, cotangent_rows).astype(BF),),
        (1,),
    )
    layer_part = dot_plain(activated, down_full).astype(BF)
    grad_resid_norm, mlp_gain_part = norm_back(grad_mlp_in, unit_mlp, inverse_mlp, mlp_gain)
    grad_residual = cotangent.astype(F32) + grad_resid_norm
    grad_branch = gather_parts(5, (grad_residual.astype(BF),))[0]
    grad_out_part = dot_first(attended, grad_branch).astype(BF)
    grad_attended = dot_last(grad_branch, out_full).astype(BF)
    grad_mixed = attend_back(
        qkv_rows, grad_attended, log_totals, cos_two, sin_two, seg_col, seg_row
    )
    grad_qkv_part = dot_first(attn_input, grad_mixed).astype(BF)
    grad_attn_in, layer_sum, qkv_grad, out_grad = reduce_sums(
        6,
        (dot_last(grad_mixed, qkv_flat).astype(BF), layer_part),
        (grad_qkv_part, grad_out_part),
        (0, 1),
    )
    layer_out = (residual + layer_sum).astype(BF)
    grad_rows_attn, attn_gain_part = norm_back(grad_attn_in, unit_attn, inverse_attn, attn_gain)
    grad_tokens = (grad_residual + grad_rows_attn).astype(BF)
    gains = sum_gains(7, jnp.stack([attn_gain_part, mlp_gain_part]).reshape(8, model_width // 4))
    gains = gains.reshape(2, model_width)
    return (
        layer_out,
        grad_tokens,
        gains[0],
        qkv_grad.reshape(qkv_weight.shape),
        out_grad,
        gains[1],
        in_grad,
        down_grad,
    )


def solution(mesh):
    fast = mesh.shape["tensor"] == 4 and mesh.shape["dp"] == 8
    chosen = fast_body if fast else body
    in_specs = (
        P(("dp", "tensor"), None),
        P(),
        P("dp", "tensor", None),
        P("tensor", "dp"),
        P(),
        P("dp", None, "tensor"),
        P("tensor", "dp"),
        P("dp", None),
        P(("dp", "tensor"), None),
    )
    out_specs = (
        P(("dp", "tensor"), None),
        P(("dp", "tensor"), None),
        P(),
        P("dp", "tensor", None),
        P("tensor", "dp"),
        P(),
        P("dp", None, "tensor"),
        P("tensor", "dp"),
    )
    return jax.shard_map(chosen, mesh=mesh, in_specs=in_specs, out_specs=out_specs, check_vma=False)
```

```python
import math

import jax
import jax.numpy as jnp
from jax import lax
from jax.experimental import pallas as pl
from jax.experimental.pallas import tpu as pltpu
from jax.sharding import PartitionSpec as P

NORM_EPS = 1e-05
ROPE_BASE = 160000.0
HALF_ROOT = 0.7071067811865476
INV_ROOT_TAU = 0.3989422804014327
MASKED_SCORE = -1e30


def dot_plain(left, right):
    return jnp.dot(left, right, preferred_element_type=jnp.float32)


def dot_first(left, right):
    return lax.dot_general(
        left, right, (((0,), (0,)), ((), ())), preferred_element_type=jnp.float32
    )


def dot_last(left, right):
    return lax.dot_general(
        left, right, (((1,), (1,)), ((), ())), preferred_element_type=jnp.float32
    )


MESH_ID = pl.DeviceIdType.MESH
VM = pltpu.VMEM
BF = jnp.bfloat16
F32 = jnp.float32
DMA = pltpu.SemaphoreType.DMA
SPLIT = 4


def swap_halves(wide):
    width = wide.shape[1]
    lane = lax.broadcasted_iota(jnp.int32, wide.shape, 1) % 64
    return jnp.where(lane < 32, pltpu.roll(wide, width - 32, 1), pltpu.roll(wide, 32, 1))


def wide_tables(cos_ref, sin_ref):
    cos_two, sin_two = cos_ref[...], sin_ref[...]
    ones, zeros = jnp.ones_like(cos_two), jnp.zeros_like(sin_two)
    return (
        jnp.concatenate([cos_two, cos_two, ones] * 2, axis=1),
        jnp.concatenate([sin_two, sin_two, zeros] * 2, axis=1),
    )


BLOCK = 256


def attend_kernel(
    reach_ref, mixed_ref, cos_ref, sin_ref, segc_ref, segr_ref, qkv_ref, att_ref, lse_ref, values_t
):
    mixed = mixed_ref[...]
    cos_wide, sin_wide = wide_tables(cos_ref, sin_ref)
    qkv_ref[...] = (mixed * cos_wide + swap_halves(mixed) * sin_wide).astype(BF)
    rows = mixed_ref.shape[0]
    for head in range(2):
        base = head * 192
        values_t[head] = qkv_ref[:, base + 128 : base + 192].astype(F32).T.astype(BF)

    def step(i, carry):
        window = pl.ds(pl.multiple_of(i * BLOCK, BLOCK), BLOCK)
        queries = [qkv_ref[window, h * 192 : h * 192 + 64] * BF(0.125) for h in range(2)]
        seg_query = segr_ref[:, window]

        def inner(j, state):
            near = pl.ds(pl.multiple_of(j * BLOCK, BLOCK), BLOCK)
            same = segc_ref[near, :] == seg_query
            after = []
            for head in range(2):
                top, total, out_t = state[3 * head : 3 * head + 3]
                base = head * 192
                scores = dot_last(qkv_ref[near, base + 64 : base + 128], queries[head])
                scores = jnp.where(same, scores, MASKED_SCORE)
                higher = jnp.maximum(top, jnp.max(scores, axis=0, keepdims=True))
                scale = jnp.exp(top - higher)
                expo = jnp.exp(scores - higher)
                after.append(higher)
                after.append(total * scale + jnp.sum(expo, axis=0, keepdims=True))
                after.append(out_t * scale + dot_plain(values_t[head, :, near], expo.astype(BF)))
            return tuple(after)

        first = (
            jnp.full((1, BLOCK), MASKED_SCORE, F32),
            jnp.zeros((1, BLOCK), F32),
            jnp.zeros((64, BLOCK), F32),
        )
        state = lax.fori_loop(reach_ref[0, i], reach_ref[1, i], inner, first * 2)
        for head in range(2):
            top, total, out_t = state[3 * head : 3 * head + 3]
            out = (out_t * (1.0 / total)).T.astype(BF)
            att_ref[window, head * 64 : head * 64 + 64] = out
            lse_ref[0, head : head + 1, window] = top + jnp.log(total)
        return carry

    lax.fori_loop(0, rows // BLOCK, step, 0)


def attend_back_kernel(
    reach_ref, qkv_ref, ga_ref, att_ref, lse_ref, cos_ref, sin_ref, segc_ref, segr_ref,
    gm_ref, acc, keys_t
):
    rows = qkv_ref.shape[0]
    for head in range(2):
        base = head * 192
        keys_t[head] = qkv_ref[:, base + 64 : base + 128].astype(F32).T.astype(BF)
    acc[...] = jnp.zeros_like(acc)

    def step(i, carry):
        window = pl.ds(pl.multiple_of(i * BLOCK, BLOCK), BLOCK)
        queries = [qkv_ref[window, h * 192 : h * 192 + 64] * BF(0.125) for h in range(2)]
        grads_o = [ga_ref[window, h * 64 : h * 64 + 64] for h in range(2)]
        seg_query = segr_ref[:, window]
        weighed = (ga_ref[window, :].astype(F32) * att_ref[window, :].astype(F32)).T
        inners = [jnp.sum(weighed[h * 64 : h * 64 + 64], axis=0, keepdims=True) for h in range(2)]
        totals = [lse_ref[0, h : h + 1, window] for h in range(2)]

        def inner(j, grads_q):
            near = pl.ds(pl.multiple_of(j * BLOCK, BLOCK), BLOCK)
            same = segc_ref[near, :] == seg_query
            after = []
            for head in range(2):
                base = head * 192
                scores = dot_last(qkv_ref[near, base + 64 : base + 128], queries[head])
                scores = jnp.where(same, scores, MASKED_SCORE)
                probs = jnp.exp(scores - totals[head])
                grad_p = dot_last(qkv_ref[near, base + 128 : base + 192], grads_o[head])
                grad_s = (probs * (grad_p - inners[head])).astype(BF)
                acc[near, base + 64 : base + 128] += dot_plain(grad_s, queries[head])
                acc[near, base + 128 : base + 192] += dot_plain(probs.astype(BF), grads_o[head])
                after.append(grads_q[head] + dot_plain(keys_t[head, :, near], grad_s))
            return tuple(after)

        empty = jnp.zeros((64, BLOCK), F32)
        grads_q = lax.fori_loop(reach_ref[0, i], reach_ref[1, i], inner, (empty, empty))
        for head in range(2):
            acc[window, head * 192 : head * 192 + 64] = (grads_q[head] * 0.125).T
        return carry

    lax.fori_loop(0, rows // BLOCK, step, 0)
    grads = acc[...]
    cos_wide, sin_wide = wide_tables(cos_ref, sin_ref)
    gm_ref[...] = (grads * cos_wide - swap_halves(grads) * sin_wide).astype(BF)


def block_reach(position):
    starts = jnp.arange(position.shape[0] // BLOCK, dtype=jnp.int32) * BLOCK
    low = (starts - position[::BLOCK]) // BLOCK
    order = jnp.arange(low.shape[0], dtype=jnp.int32)
    high = jnp.sum((low[None, :] <= order[:, None]).astype(jnp.int32), axis=1)
    return jnp.stack([low, high])


def attend(reach, mixed, cos_two, sin_two, seg_col, seg_row):
    rows, cols = mixed.shape
    pairs = cols // 384
    whole = lambda p: (0, 0)
    return pl.pallas_call(
        attend_kernel,
        grid=(pairs,),
        in_specs=[
            pl.BlockSpec(memory_space=pltpu.SMEM),
            pl.BlockSpec((rows, 384), lambda p: (0, p)),
            pl.BlockSpec((rows, 64), whole),
            pl.BlockSpec((rows, 64), whole),
            pl.BlockSpec((rows, 1), whole),
            pl.BlockSpec((1, rows), whole),
        ],
        out_specs=[
            pl.BlockSpec((rows, 384), lambda p: (0, p)),
            pl.BlockSpec((rows, 128), lambda p: (0, p)),
            pl.BlockSpec((1, 2, rows), lambda p: (p, 0, 0)),
        ],
        out_shape=[
            jax.ShapeDtypeStruct((rows, cols), BF),
            jax.ShapeDtypeStruct((rows, pairs * 128), BF),
            jax.ShapeDtypeStruct((pairs, 2, rows), F32),
        ],
        scratch_shapes=[VM((2, 64, rows), BF)],
        cost_estimate=pl.CostEstimate(
            flops=pairs * 2 * rows * rows * 64 * 4,
            transcendentals=pairs * 2 * rows * rows,
            bytes_accessed=rows * cols * 8,
        ),
        compiler_params=pltpu.CompilerParams(vmem_limit_bytes=48 << 20),
        name="attend",
    )(reach, mixed, cos_two, sin_two, seg_col, seg_row)


def attend_back(reach, qkv, grad_att, attended, lse, cos_two, sin_two, seg_col, seg_row):
    rows, cols = qkv.shape
    pairs = cols // 384
    whole = lambda p: (0, 0)
    return pl.pallas_call(
        attend_back_kernel,
        grid=(pairs,),
        in_specs=[
            pl.BlockSpec(memory_space=pltpu.SMEM),
            pl.BlockSpec((rows, 384), lambda p: (0, p)),
            pl.BlockSpec((rows, 128), lambda p: (0, p)),
            pl.BlockSpec((rows, 128), lambda p: (0, p)),
            pl.BlockSpec((1, 2, rows), lambda p: (p, 0, 0)),
            pl.BlockSpec((rows, 64), whole),
            pl.BlockSpec((rows, 64), whole),
            pl.BlockSpec((rows, 1), whole),
            pl.BlockSpec((1, rows), whole),
        ],
        out_specs=pl.BlockSpec((rows, 384), lambda p: (0, p)),
        out_shape=jax.ShapeDtypeStruct((rows, cols), BF),
        scratch_shapes=[VM((rows, 384), F32), VM((2, 64, rows), BF)],
        cost_estimate=pl.CostEstimate(
            flops=pairs * 2 * rows * rows * 64 * 10,
            transcendentals=pairs * 2 * rows * rows,
            bytes_accessed=rows * cols * 8,
        ),
        compiler_params=pltpu.CompilerParams(vmem_limit_bytes=48 << 20),
        name="attend_back",
    )(reach, qkv, grad_att, attended, lse, cos_two, sin_two, seg_col, seg_row)


def remote(source, target, send_sem, recv_sem, device):
    return pltpu.make_async_remote_copy(
        src_ref=source, dst_ref=target, send_sem=send_sem, recv_sem=recv_sem,
        device_id=device, device_id_type=MESH_ID,
    )


def greet(peers):
    barrier = pltpu.get_barrier_semaphore()
    for peer in peers:
        pl.semaphore_signal(barrier, inc=1, device_id=peer, device_id_type=MESH_ID)
    pl.semaphore_wait(barrier, len(peers))


def near_peers():
    dp, mine = lax.axis_index("dp"), lax.axis_index("tensor")
    across = (mine + 2) % 4
    beside = mine + 1 - 2 * (mine % 2)
    return dp, mine, across, beside


def far_peers():
    dp, mine = lax.axis_index("dp"), lax.axis_index("tensor")
    level, side = dp // 2, dp % 2
    cross = dp + 1 - 2 * side
    ahead = [((level + k) % 4) * 2 + side for k in range(4)]
    behind = [((level + 4 - k) % 4) * 2 + side for k in range(4)]
    return dp, mine, cross, ahead, behind


class RowGather:
    sems = [DMA((SPLIT,)), DMA((SPLIT,)), DMA((SPLIT + 1,)), DMA((SPLIT + 1,)), DMA]

    def __init__(self, source, target, sems):
        self.source, self.target, self.sems_in = source, target, sems
        self.rows = source.shape[0]

    def start(self):
        dp, mine, across, beside = near_peers()
        send_y, recv_y, send_c, recv_c, own = self.sems_in
        rows, part = self.rows, self.rows // SPLIT
        self.links = []
        for j in range(SPLIT):
            link = remote(
                self.source.at[pl.ds(j * part, part)],
                self.target.at[pl.ds(mine * rows + j * part, part)],
                send_y.at[j], recv_y.at[j], (dp, across))
            link.start()
            self.links.append(link)
        self.beside = remote(
            self.source, self.target.at[pl.ds(mine * rows, rows)],
            send_c.at[SPLIT], recv_c.at[SPLIT], (dp, beside))
        self.beside.start()
        self.local = pltpu.make_async_copy(
            self.source, self.target.at[pl.ds(mine * rows, rows)], own)
        self.local.start()
        self.forwards = []

    def step(self, j):
        dp, mine, across, beside = near_peers()
        send_y, recv_y, send_c, recv_c, own = self.sems_in
        rows, part = self.rows, self.rows // SPLIT
        place = self.target.at[pl.ds(across * rows + j * part, part)]
        remote(self.source.at[pl.ds(j * part, part)], place,
               send_y.at[j], recv_y.at[j], (dp, across)).wait_recv()
        forward = remote(place, place, send_c.at[j], recv_c.at[j], (dp, beside))
        forward.start()
        self.forwards.append(forward)

    def finish(self):
        dp, mine, across, beside = near_peers()
        send_y, recv_y, send_c, recv_c, own = self.sems_in
        rows, part = self.rows, self.rows // SPLIT
        other = beside
        remote(self.source, self.target.at[pl.ds(other * rows, rows)],
               send_c.at[SPLIT], recv_c.at[SPLIT], (dp, beside)).wait_recv()
        diagonal = (beside + 2) % 4
        for j in range(SPLIT):
            place = self.target.at[pl.ds(diagonal * rows + j * part, part)]
            remote(place, place, send_c.at[j], recv_c.at[j], (dp, beside)).wait_recv()
        for link in self.links + self.forwards + [self.beside]:
            link.wait_send()
        self.local.wait()


class WeightGather:
    sems = [DMA((8,)), DMA((8,)), DMA]

    def __init__(self, source, target, sems, axis):
        self.source, self.target, self.sems_in, self.axis = source, target, sems, axis

    def place(self, index):
        size = self.source.shape[self.axis]
        window = pl.ds(pl.multiple_of(index * size, size), size)
        return self.target.at[window] if self.axis == 0 else self.target.at[:, window]

    def start(self):
        dp, mine, cross, ahead, behind = far_peers()
        send, recv, own = self.sems_in
        self.links = []
        for k in (2, 1, 3):
            link = remote(self.source, self.place(dp), send.at[k], recv.at[k], (ahead[k], mine))
            link.start()
            self.links.append(link)
        link = remote(self.source, self.place(dp), send.at[4], recv.at[4], (cross, mine))
        link.start()
        self.links.append(link)
        self.local = pltpu.make_async_copy(self.source, self.place(dp), own)
        self.local.start()

    def step(self, k):
        dp, mine, cross, ahead, behind = far_peers()
        send, recv, own = self.sems_in
        place = self.place(behind[k])
        remote(self.source, place, send.at[k], recv.at[k], (ahead[k], mine)).wait_recv()
        link = remote(place, place, send.at[4 + k], recv.at[4 + k], (cross, mine))
        link.start()
        self.links.append(link)

    def finish(self):
        dp, mine, cross, ahead, behind = far_peers()
        send, recv, own = self.sems_in
        for k in range(4):
            index = behind[k] + 1 - 2 * (dp % 2)
            place = self.place(index)
            remote(place, place, send.at[4 + k], recv.at[4 + k], (cross, mine)).wait_recv()
        for link in self.links:
            link.wait_send()
        self.local.wait()


class RowReduce:
    sems = [DMA((SPLIT + 1,)), DMA((SPLIT + 1,)), DMA((SPLIT,)), DMA((SPLIT,))]

    @staticmethod
    def scratch(rows, width):
        return [VM((rows, width), BF), VM((rows, width), BF), VM((rows, width), BF), VM((rows, width), BF)]

    def __init__(self, source, target, scratch, sems):
        self.source, self.target, self.scratch_in, self.sems_in = source, target, scratch, sems
        self.rows = target.shape[0]

    def start(self):
        dp, mine, across, beside = near_peers()
        send_c, recv_c, send_y, recv_y = self.sems_in
        far_in, near_in, sums, y_in = self.scratch_in
        rows, part = self.rows, self.rows // SPLIT
        diagonal = (beside + 2) % 4
        self.links = []
        for j in range(SPLIT):
            link = remote(
                self.source.at[pl.ds(diagonal * rows + j * part, part)],
                far_in.at[pl.ds(j * part, part)], send_c.at[j], recv_c.at[j], (dp, beside))
            link.start()
            self.links.append(link)
        link = remote(
            self.source.at[pl.ds(beside * rows, rows)], near_in,
            send_c.at[SPLIT], recv_c.at[SPLIT], (dp, beside))
        link.start()
        self.links.append(link)

    def step(self, j):
        dp, mine, across, beside = near_peers()
        send_c, recv_c, send_y, recv_y = self.sems_in
        far_in, near_in, sums, y_in = self.scratch_in
        rows, part = self.rows, self.rows // SPLIT
        window = pl.ds(j * part, part)
        self.links[j].wait_recv()
        sums[window] = (
            self.source[pl.ds(across * rows + j * part, part)].astype(F32)
            + far_in[window].astype(F32)
        ).astype(BF)
        link = remote(sums.at[window], y_in.at[window], send_y.at[j], recv_y.at[j], (dp, across))
        link.start()
        self.links.append(link)

    def finish(self):
        dp, mine, across, beside = near_peers()
        far_in, near_in, sums, y_in = self.scratch_in
        rows, part = self.rows, self.rows // SPLIT
        self.links[SPLIT].wait_recv()
        for j in range(SPLIT):
            window = pl.ds(j * part, part)
            self.links[SPLIT + 1 + j].wait_recv()
            self.target[window] = (
                self.source[pl.ds(mine * rows + j * part, part)].astype(F32)
                + near_in[window].astype(F32)
                + y_in[window].astype(F32)
            )
        for link in self.links:
            link.wait_send()


class WeightReduce:
    sems = [DMA((8,)), DMA((8,))]

    @staticmethod
    def scratch(shape):
        return [VM((4, *shape), BF), VM((4, *shape), BF), VM((4, *shape), BF)]

    def __init__(self, source, target, scratch, sems, axis):
        self.source, self.target, self.scratch_in, self.sems_in = source, target, scratch, sems
        self.axis = axis

    def window(self, index):
        size = self.target.shape[self.axis]
        window = pl.ds(pl.multiple_of(index * size, size), size)
        return (window,) if self.axis == 0 else (slice(None), window)

    def start(self):
        dp, mine, cross, ahead, behind = far_peers()
        send, recv = self.sems_in
        x_in, sums, z_in = self.scratch_in
        self.links = {}
        for k in (2, 1, 3, 0):
            index = ahead[k] + 1 - 2 * (dp % 2)
            link = remote(self.source.at[self.window(index)], x_in.at[k],
                          send.at[k], recv.at[k], (cross, mine))
            link.start()
            self.links[k] = link

    def step(self, k):
        dp, mine, cross, ahead, behind = far_peers()
        send, recv = self.sems_in
        x_in, sums, z_in = self.scratch_in
        self.links[k].wait_recv()
        sums[k] = (self.source[self.window(ahead[k])].astype(F32) + x_in[k].astype(F32)).astype(BF)
        if k:
            link = remote(sums.at[k], z_in.at[k], send.at[4 + k], recv.at[4 + k], (ahead[k], mine))
            link.start()
            self.links[4 + k] = link

    def finish(self):
        x_in, sums, z_in = self.scratch_in
        for k in (1, 2, 3):
            self.links[4 + k].wait_recv()
        self.target[...] = (
            sums[0].astype(F32) + z_in[1].astype(F32) + z_in[2].astype(F32) + z_in[3].astype(F32)
        )
        for link in self.links.values():
            link.wait_send()


def run_parts(near, far):
    dp, mine, across, beside = near_peers()
    peers = [(dp, across), (dp, beside)] if near else []
    if far:
        dp, mine, cross, ahead, behind = far_peers()
        peers += [(cross, mine)] + [(ahead[k], mine) for k in (1, 2, 3)]
    greet(peers)
    for part in near + far:
        part.start()
    for j in range(SPLIT):
        for part in near:
            part.step(j)
        for part in far:
            k = (2, 1, 3, 0)[j]
            if k or isinstance(part, WeightReduce):
                part.step(k)
    for part in near + far:
        part.finish()


def comm_call(kernel, args, outs, out_spaces, scratch, ident, name):
    return pl.pallas_call(
        kernel,
        out_shape=[jax.ShapeDtypeStruct(*out) for out in outs],
        in_specs=[pl.BlockSpec(memory_space=VM)] * len(args),
        out_specs=[pl.BlockSpec(memory_space=space) for space in out_spaces],
        scratch_shapes=scratch,
        compiler_params=pltpu.CompilerParams(
            collective_id=ident, has_side_effects=True, vmem_limit_bytes=40 << 20
        ),
        name=name,
    )(*args)


def gather_parts(ident, rows, weights=(), axes=()):
    near_count, count = len(rows), len(rows) + len(weights)
    per_row, per_weight = len(RowGather.sems), len(WeightGather.sems)

    def kernel(*refs):
        ins, outs, sems = refs[:count], refs[count : 2 * count], refs[2 * count :]
        near = [
            RowGather(ins[i], outs[i], sems[i * per_row : (i + 1) * per_row])
            for i in range(near_count)
        ]
        sems = sems[near_count * per_row :]
        far = [
            WeightGather(
                ins[near_count + i], outs[near_count + i],
                sems[i * per_weight : (i + 1) * per_weight], axes[i])
            for i in range(len(weights))
        ]
        run_parts(near, far)

    shapes = [((4 * a.shape[0], a.shape[1]), BF) for a in rows]
    for weight, axis in zip(weights, axes):
        shape = list(weight.shape)
        shape[axis] = shape[axis] * 8
        shapes.append((tuple(shape), BF))
    return comm_call(
        kernel, (*rows, *weights), shapes, [pl.ANY] * count,
        RowGather.sems * near_count + WeightGather.sems * len(weights), ident, "gather_parts")


def reduce_sums(ident, partials, grads=(), axes=()):
    near_count, count = len(partials), len(partials) + len(grads)
    shapes, scratch = [], []
    for partial in partials:
        shape = (partial.shape[0] // 4, partial.shape[1])
        shapes.append((shape, F32))
        scratch = scratch + RowReduce.scratch(*shape) + RowReduce.sems
    for grad, axis in zip(grads, axes):
        shape = list(grad.shape)
        shape[axis] = shape[axis] // 8
        shapes.append((tuple(shape), F32))
        scratch = scratch + WeightReduce.scratch(tuple(shape)) + WeightReduce.sems

    def kernel(*refs):
        ins, outs, rest = refs[:count], refs[count : 2 * count], refs[2 * count :]
        near = []
        for i in range(near_count):
            near.append(RowReduce(ins[i], outs[i], rest[:4], rest[4:8]))
            rest = rest[8:]
        far = []
        for i in range(len(grads)):
            far.append(WeightReduce(ins[near_count + i], outs[near_count + i], rest[:3], rest[3:5], axes[i]))
            rest = rest[5:]
        run_parts(near, far)

    return comm_call(kernel, (*partials, *grads), shapes, [VM] * count, scratch, ident, "reduce_sums")


def sum_gains_kernel(part_ref, out_ref, near_in, mid, far_in, send_n, recv_n, send_f, recv_f):
    dp, mine = lax.axis_index("dp"), lax.axis_index("tensor")
    near = [(dp, (mine + k) % 4) for k in range(1, 4)]
    far = [((dp + k) % 8, mine) for k in range(1, 8)]
    greet(near + far)
    links = []
    for k in range(3):
        link = remote(part_ref, near_in.at[k], send_n.at[k], recv_n.at[k], near[k])
        link.start()
        links.append(link)
    for link in links:
        link.wait_recv()
    mid[...] = part_ref[...] + near_in[0] + near_in[1] + near_in[2]
    more = []
    for k in range(7):
        link = remote(mid, far_in.at[k], send_f.at[k], recv_f.at[k], far[k])
        link.start()
        more.append(link)
    total = mid[...]
    for k in range(7):
        more[k].wait_recv()
        total = total + far_in[k]
    out_ref[...] = total
    for link in links + more:
        link.wait_send()


def sum_gains(ident, parts):
    shape = parts.shape
    return comm_call(
        sum_gains_kernel, (parts,), [(shape, F32)], [VM],
        [VM((3, *shape), F32), VM(shape, F32), VM((7, *shape), F32),
         DMA((3,)), DMA((3,)), DMA((7,)), DMA((7,))], ident, "sum_gains")[0]


def layer_norm(row_data, norm_gain):
    centered = row_data - jnp.mean(row_data, axis=-1, keepdims=True)
    inverse = lax.rsqrt(jnp.mean(centered * centered, axis=-1, keepdims=True) + NORM_EPS)
    unit_rows = centered * inverse
    return (unit_rows * norm_gain, unit_rows, inverse)


def norm_back(grad_normed, unit_rows, inverse, norm_gain):
    scaled = grad_normed * norm_gain
    grad_rows = inverse * (
        scaled
        - jnp.mean(scaled, axis=-1, keepdims=True)
        - unit_rows * jnp.mean(scaled * unit_rows, axis=-1, keepdims=True)
    )
    return (grad_rows, jnp.sum(grad_normed * unit_rows, axis=0))


def gelu_parts(value_in):
    normal_cdf = 0.5 * (1.0 + lax.erf(value_in * HALF_ROOT))
    slope = normal_cdf + value_in * INV_ROOT_TAU * jnp.exp(-0.5 * value_in * value_in)
    return (value_in * normal_cdf, slope)


def segment_info(seg_lens, pack_rows):
    seg_ends = jnp.cumsum(seg_lens)
    places = lax.iota(jnp.int32, pack_rows)
    before = seg_ends[None, :] <= places[:, None]
    seg_ids = jnp.sum(before.astype(jnp.int32), axis=1)
    seg_first = jnp.sum(jnp.where(before, seg_lens[None, :], 0), axis=1)
    return (seg_ids, places - seg_first)


def rotary(position, head_dim):
    half_dim = head_dim // 2
    inv_freq = jnp.exp(lax.iota(jnp.float32, half_dim) * (-2.0 * math.log(ROPE_BASE) / head_dim))
    angles = position.astype(jnp.float32)[:, None] * inv_freq[None, :]
    return (jnp.cos(angles), jnp.sin(angles))


def turn(vectors, cos_table, sin_table):
    half_dim = vectors.shape[-1] // 2
    front_half = vectors[..., :half_dim]
    back_half = vectors[..., half_dim:]
    cos_part = cos_table[:, None, :]
    sin_part = sin_table[:, None, :]
    return jnp.concatenate(
        [
            front_half * cos_part - back_half * sin_part,
            back_half * cos_part + front_half * sin_part,
        ],
        axis=-1,
    )


def turn_back(grads_in, cos_table, sin_table):
    half_dim = grads_in.shape[-1] // 2
    front_half = grads_in[..., :half_dim]
    back_half = grads_in[..., half_dim:]
    cos_part = cos_table[:, None, :]
    sin_part = sin_table[:, None, :]
    return jnp.concatenate(
        [
            front_half * cos_part + back_half * sin_part,
            back_half * cos_part - front_half * sin_part,
        ],
        axis=-1,
    )


def block_scores(query_part, key_part, seg_query, seg_key, score_scale):
    scores = (
        jnp.einsum("qhd,khd->hqk", query_part, key_part, preferred_element_type=jnp.float32)
        * score_scale
    )
    return jnp.where((seg_query[:, None] == seg_key[None, :])[None], scores, MASKED_SCORE)


def attention_forward(query_rows, key_rows, value_rows, seg_ids, query_block, score_scale):
    pack_rows, heads_local, head_dim = query_rows.shape
    block_count = pack_rows // query_block

    def one_block(block_index):
        query_start = block_index * query_block
        query_part = lax.dynamic_slice_in_dim(query_rows, query_start, query_block, 0)
        seg_query = lax.dynamic_slice_in_dim(seg_ids, query_start, query_block, 0)
        scores = block_scores(query_part, key_rows, seg_query, seg_ids, score_scale)
        row_top = jnp.max(scores, axis=-1, keepdims=True)
        expo = jnp.exp(scores - row_top)
        row_total = jnp.sum(expo, axis=-1, keepdims=True)
        weights = (expo / row_total).astype(jnp.bfloat16)
        result = jnp.einsum("hqk,khd->qhd", weights, value_rows, preferred_element_type=jnp.float32)
        return (result, (row_top + jnp.log(row_total))[..., 0])

    results, log_totals = lax.map(one_block, jnp.arange(block_count, dtype=jnp.int32))
    return (results.reshape(pack_rows, heads_local, head_dim), log_totals)


def attention_backward(
    query_rows, key_rows, value_rows, grad_attended, log_totals, seg_ids, query_block, score_scale
):
    pack_rows, heads_local, head_dim = query_rows.shape
    block_count = pack_rows // query_block

    def block_step(running, block_index):
        grad_keys, grad_values = running
        query_start = block_index * query_block
        query_part = lax.dynamic_slice_in_dim(query_rows, query_start, query_block, 0)
        grad_part = lax.dynamic_slice_in_dim(grad_attended, query_start, query_block, 0)
        seg_query = lax.dynamic_slice_in_dim(seg_ids, query_start, query_block, 0)
        scores = block_scores(query_part, key_rows, seg_query, seg_ids, score_scale)
        probs = jnp.exp(scores - log_totals[block_index][..., None])
        grad_probs = jnp.einsum(
            "qhd,khd->hqk", grad_part, value_rows, preferred_element_type=jnp.float32
        )
        inner = jnp.sum(probs * grad_probs, axis=-1, keepdims=True)
        grad_scores = (probs * (grad_probs - inner)).astype(jnp.bfloat16) * score_scale
        grad_query_part = jnp.einsum(
            "hqk,khd->qhd", grad_scores, key_rows, preferred_element_type=jnp.float32
        )
        grad_key_part = jnp.einsum(
            "hqk,qhd->khd", grad_scores, query_part, preferred_element_type=jnp.float32
        )
        grad_value_part = jnp.einsum(
            "hqk,qhd->khd",
            probs.astype(jnp.bfloat16),
            grad_part,
            preferred_element_type=jnp.float32,
        )
        grad_keys = grad_keys + grad_key_part
        grad_values = grad_values + grad_value_part
        return ((grad_keys, grad_values), grad_query_part)

    empty_grad = jnp.zeros(query_rows.shape, jnp.float32)
    (grad_keys, grad_values), grad_queries = lax.scan(
        block_step, (empty_grad, empty_grad), jnp.arange(block_count, dtype=jnp.int32)
    )
    return (grad_queries.reshape(pack_rows, heads_local, head_dim), grad_keys, grad_values)


def body(
    tokens,
    attn_gain,
    qkv_weight,
    out_weight,
    mlp_gain,
    in_weight,
    down_weight,
    seg_lengths,
    cotangent,
):
    tok_dev, model_width = tokens.shape
    pack_rows = tok_dev * lax.axis_size("tensor")
    heads_local = qkv_weight.shape[1]
    head_dim = qkv_weight.shape[2] // 3
    hidden_local = in_weight.shape[2]
    score_scale = head_dim ** (-0.5)
    query_block = min(512, pack_rows)
    qkv_full, out_full, in_full, down_full = (
        lax.all_gather(qkv_weight, "dp", axis=0, tiled=True),
        lax.all_gather(out_weight, "dp", axis=1, tiled=True),
        lax.all_gather(in_weight, "dp", axis=0, tiled=True),
        lax.all_gather(down_weight, "dp", axis=1, tiled=True),
    )
    qkv_flat = qkv_full.reshape(model_width, heads_local * 3 * head_dim)
    seg_ids, position = segment_info(seg_lengths[0], pack_rows)
    cos_table, sin_table = rotary(position, head_dim)
    row_data = tokens.astype(jnp.float32)
    normed_attn, unit_attn, inverse_attn = layer_norm(row_data, attn_gain)
    attn_input = lax.all_gather(normed_attn.astype(jnp.bfloat16), "tensor", axis=0, tiled=True)
    mixed_proj = dot_plain(attn_input, qkv_flat).reshape(pack_rows, heads_local, 3, head_dim)
    query_rows = turn(mixed_proj[:, :, 0], cos_table, sin_table).astype(jnp.bfloat16)
    key_rows = turn(mixed_proj[:, :, 1], cos_table, sin_table).astype(jnp.bfloat16)
    value_rows = mixed_proj[:, :, 2].astype(jnp.bfloat16)
    attended, log_totals = attention_forward(
        query_rows, key_rows, value_rows, seg_ids, query_block, score_scale
    )
    attended = attended.reshape(pack_rows, heads_local * head_dim).astype(jnp.bfloat16)
    residual = row_data + lax.psum_scatter(
        dot_plain(attended, out_full).astype(jnp.bfloat16),
        "tensor",
        scatter_dimension=0,
        tiled=True,
    ).astype(jnp.float32)
    normed_mlp, unit_mlp, inverse_mlp = layer_norm(residual, mlp_gain)
    mlp_input = normed_mlp.astype(jnp.bfloat16)
    mlp_rows = lax.all_gather(mlp_input, "tensor", axis=0, tiled=True)
    in_flat = in_full.reshape(model_width, -1)
    lifted = dot_plain(mlp_rows, in_flat).reshape(pack_rows, 2, hidden_local)
    act_gelu, act_slope = gelu_parts(lifted[:, 0])
    activated = (act_gelu * lifted[:, 1]).astype(jnp.bfloat16)
    layer_out = (
        residual
        + lax.psum_scatter(
            dot_plain(activated, down_full).astype(jnp.bfloat16),
            "tensor",
            scatter_dimension=0,
            tiled=True,
        ).astype(jnp.float32)
    ).astype(jnp.bfloat16)
    cotangent_rows = lax.all_gather(cotangent, "tensor", axis=0, tiled=True)
    grad_act = dot_last(cotangent_rows, down_full)
    grad_lifted = jnp.concatenate(
        [grad_act * lifted[:, 1] * act_slope, grad_act * act_gelu], axis=1
    ).astype(jnp.bfloat16)
    grad_mlp_in = lax.psum_scatter(
        dot_last(grad_lifted, in_flat).astype(jnp.bfloat16),
        "tensor",
        scatter_dimension=0,
        tiled=True,
    ).astype(jnp.float32)
    grad_in_part = dot_first(mlp_rows, grad_lifted).reshape(in_full.shape)
    grad_down_part = dot_first(activated, cotangent_rows)
    grad_resid_norm, mlp_gain_part = norm_back(grad_mlp_in, unit_mlp, inverse_mlp, mlp_gain)
    grad_residual = cotangent.astype(jnp.float32) + grad_resid_norm
    grad_branch = lax.all_gather(grad_residual.astype(jnp.bfloat16), "tensor", axis=0, tiled=True)
    grad_out_part = dot_first(attended, grad_branch)
    grad_attended = (
        dot_last(grad_branch, out_full)
        .astype(jnp.bfloat16)
        .reshape(pack_rows, heads_local, head_dim)
    )
    grad_queries, grad_keys, grad_values = attention_backward(
        query_rows,
        key_rows,
        value_rows,
        grad_attended,
        log_totals,
        seg_ids,
        query_block,
        score_scale,
    )
    grad_mixed = jnp.stack(
        [
            turn_back(grad_queries, cos_table, sin_table),
            turn_back(grad_keys, cos_table, sin_table),
            grad_values,
        ],
        axis=2,
    )
    grad_mixed = grad_mixed.reshape(pack_rows, heads_local * 3 * head_dim).astype(jnp.bfloat16)
    grad_qkv_part = dot_first(attn_input, grad_mixed).reshape(qkv_full.shape)
    grad_attn_in = lax.psum_scatter(
        dot_last(grad_mixed, qkv_flat).astype(jnp.bfloat16),
        "tensor",
        scatter_dimension=0,
        tiled=True,
    ).astype(jnp.float32)
    grad_rows_attn, attn_gain_part = norm_back(grad_attn_in, unit_attn, inverse_attn, attn_gain)
    grad_tokens = (grad_residual + grad_rows_attn).astype(jnp.bfloat16)
    qkv_grad, out_grad, in_grad, down_grad = (
        lax.psum_scatter(
            grad_qkv_part.astype(jnp.bfloat16), "dp", scatter_dimension=0, tiled=True
        ).astype(jnp.float32),
        lax.psum_scatter(
            grad_out_part.astype(jnp.bfloat16), "dp", scatter_dimension=1, tiled=True
        ).astype(jnp.float32),
        lax.psum_scatter(
            grad_in_part.astype(jnp.bfloat16), "dp", scatter_dimension=0, tiled=True
        ).astype(jnp.float32),
        lax.psum_scatter(
            grad_down_part.astype(jnp.bfloat16), "dp", scatter_dimension=1, tiled=True
        ).astype(jnp.float32),
    )
    attn_gain_grad, mlp_gain_grad = lax.psum((attn_gain_part, mlp_gain_part), ("dp", "tensor"))
    return (
        layer_out,
        grad_tokens,
        attn_gain_grad,
        qkv_grad,
        out_grad,
        mlp_gain_grad,
        in_grad,
        down_grad,
    )


def fast_body(
    tokens,
    attn_gain,
    qkv_weight,
    out_weight,
    mlp_gain,
    in_weight,
    down_weight,
    seg_lengths,
    cotangent,
):
    tok_dev, model_width = tokens.shape
    pack_rows = tok_dev * 4
    heads_local = qkv_weight.shape[1]
    head_dim = qkv_weight.shape[2] // 3
    hidden_local = in_weight.shape[2]
    row_data = tokens.astype(F32)
    normed_attn, unit_attn, inverse_attn = layer_norm(row_data, attn_gain)
    attn_input, cotangent_rows, qkv_flat, out_full = gather_parts(
        1,
        (normed_attn.astype(BF), cotangent),
        (qkv_weight.reshape(qkv_weight.shape[0], heads_local * 3 * head_dim), out_weight),
        (0, 1),
    )
    in_shard = in_weight.reshape(in_weight.shape[0], 2 * hidden_local)
    in_shard, attn_input = lax.optimization_barrier((in_shard, attn_input))
    in_flat = lax.all_gather(in_shard, "dp", axis=0, tiled=True)
    seg_ids, position = segment_info(seg_lengths[0], pack_rows)
    cos_table, sin_table = rotary(position, head_dim)
    cos_two = jnp.concatenate([cos_table, cos_table], axis=1)
    sin_two = jnp.concatenate([-sin_table, sin_table], axis=1)
    seg_col, seg_row = seg_ids[:, None], seg_ids[None, :]
    reach = block_reach(position)
    mixed_proj = dot_plain(attn_input, qkv_flat)
    qkv_rows, attended, log_totals = attend(reach, mixed_proj, cos_two, sin_two, seg_col, seg_row)
    residual = row_data + reduce_sums(2, (dot_plain(attended, out_full).astype(BF),))[0]
    normed_mlp, unit_mlp, inverse_mlp = layer_norm(residual, mlp_gain)
    mlp_rows, down_full = gather_parts(3, (normed_mlp.astype(BF),), (down_weight,), (1,))
    lifted = dot_plain(mlp_rows, in_flat)
    gate = lifted[:, hidden_local:]
    act_gelu, act_slope = gelu_parts(lifted[:, :hidden_local])
    activated = (act_gelu * gate).astype(BF)
    grad_act = dot_last(cotangent_rows, down_full)
    grad_lifted = jnp.concatenate(
        [grad_act * gate * act_slope, grad_act * act_gelu], axis=1
    ).astype(BF)
    in_grad = lax.psum_scatter(
        dot_first(mlp_rows, grad_lifted).astype(BF), "dp", scatter_dimension=0, tiled=True
    )
    in_grad = in_grad.reshape(in_weight.shape).astype(F32)
    grad_mlp_in, down_grad = reduce_sums(
        4,
        (dot_last(grad_lifted, in_flat).astype(BF),),
        (dot_first(activated, cotangent_rows).astype(BF),),
        (1,),
    )
    layer_part = dot_plain(activated, down_full).astype(BF)
    grad_resid_norm, mlp_gain_part = norm_back(grad_mlp_in, unit_mlp, inverse_mlp, mlp_gain)
    grad_residual = cotangent.astype(F32) + grad_resid_norm
    grad_branch = gather_parts(5, (grad_residual.astype(BF),))[0]
    grad_out_part = dot_first(attended, grad_branch).astype(BF)
    grad_attended = dot_last(grad_branch, out_full).astype(BF)
    grad_mixed = attend_back(
        reach, qkv_rows, grad_attended, attended, log_totals, cos_two, sin_two, seg_col, seg_row
    )
    grad_qkv_part = dot_first(attn_input, grad_mixed).astype(BF)
    grad_attn_in, layer_sum, qkv_grad, out_grad = reduce_sums(
        6,
        (dot_last(grad_mixed, qkv_flat).astype(BF), layer_part),
        (grad_qkv_part, grad_out_part),
        (0, 1),
    )
    layer_out = (residual + layer_sum).astype(BF)
    grad_rows_attn, attn_gain_part = norm_back(grad_attn_in, unit_attn, inverse_attn, attn_gain)
    grad_tokens = (grad_residual + grad_rows_attn).astype(BF)
    gains = sum_gains(7, jnp.stack([attn_gain_part, mlp_gain_part]).reshape(8, model_width // 4))
    gains = gains.reshape(2, model_width)
    return (
        layer_out,
        grad_tokens,
        gains[0],
        qkv_grad.reshape(qkv_weight.shape),
        out_grad,
        gains[1],
        in_grad,
        down_grad,
    )


def solution(mesh):
    fast = mesh.shape["tensor"] == 4 and mesh.shape["dp"] == 8
    chosen = fast_body if fast else body
    in_specs = (
        P(("dp", "tensor"), None),
        P(),
        P("dp", "tensor", None),
        P("tensor", "dp"),
        P(),
        P("dp", None, "tensor"),
        P("tensor", "dp"),
        P("dp", None),
        P(("dp", "tensor"), None),
    )
    out_specs = (
        P(("dp", "tensor"), None),
        P(("dp", "tensor"), None),
        P(),
        P("dp", "tensor", None),
        P("tensor", "dp"),
        P(),
        P("dp", None, "tensor"),
        P("tensor", "dp"),
    )
    return jax.shard_map(chosen, mesh=mesh, in_specs=in_specs, out_specs=out_specs, check_vma=False)
```
